32 devices in a mesh: group: 2 (over x), dp: 16 (over z, y, core).
Axes of the slice: x: 2, y: 2, z: 4, core: 2. Of those that a mesh axis runs over, the one named last changes fastest.
Arguments:
- candidate_queries: bfloat16 [256, 8, 16, 4096], P(('group', 'dp')), parts along dimension 0, may hold values from -10 to 10
- target_states: bfloat16 [256, 32, 1024], P(('group', 'dp')), parts along dimension 0, may hold values from -4 to 4
- target_queries: bfloat16 [256, 32, 4096], P(('group', 'dp')), parts along dimension 0, may hold values from -10 to 10
- candidate_states: bfloat16 [2048, 16, 1024], P(('group', 'dp')), parts along dimension 0, may hold values from -4 to 4
- target_length: int32 [256], P(('group', 'dp')), parts along dimension 0, may hold values from 2 to 32
- candidate_length: int32 [256, 8], P(('group', 'dp')), parts along dimension 0, may hold values from 2 to 16
- candidate_row: int32 [256, 8], P(('group', 'dp')), parts along dimension 0, may hold values from 0 to 63, as said below
- direct_readout: bfloat16 [4096], replicated, may hold values from -0.5 to 0.5
- channel_readout: bfloat16 [4096], replicated, may hold values from -0.5 to 0.5
Outputs:
- rescored: float32 [2048], P(('group', 'dp')), parts along dimension 0
The draws below stay inside these ranges and needn't reach their ends.
There are 2 independent parts, one for each index of `group`. The reference program is written for one: setup_inputs(seed, part) draws one part's arguments, and reference() takes and returns one part's arrays. A program takes and returns all parts, laid end to end along the dimension named above; an argument that names none is the same for every part. Nothing has to cross between parts.
Inputs may be any that keep to these rules, and one draw needn't show every extreme that they name: `candidate_row`: on the 8 targets of each aligned block (targets b * 8 to (b + 1) * 8 - 1), the 64 entries hold every value from 0 to 63 once.
All inputs are finite; a program needn't handle non-finite values.
Results may differ from the reference program's by a relative error of at most 0.0021.
Values may be sent and summed in bfloat16 or wider, within the bound.
A program may use at most 128 MiB of HBM per device.

```python
import math
import jax
import jax.numpy as jnp
from jax import lax

TGT_DEV = 8
SLOTS = 8
TARGET_TOKENS = 32
SOURCE_TOKENS = 16
QUERY_HEADS = 32
KEY_VALUE_HEADS = 4
HEAD_SIZE = 128
QW = 4096
PART_TARGETS = 128
CAND_DEV = 64
CANDIDATE_PAIRS = 1024
PEER_ROWS = 4


def starting_values(key, shape):
    return jax.random.truncated_normal(jax.random.fold_in(key, 3), -4.0, 4.0, shape)


def draw_candidate_queries(key, part):
    value_rows = starting_values(jax.random.fold_in(key, 21), (PART_TARGETS, SLOTS, SOURCE_TOKENS, QUERY_HEADS * HEAD_SIZE))
    return value_rows.astype(jnp.bfloat16)


def draw_target_states(key, part):
    value_rows = starting_values(jax.random.fold_in(key, 22), (PART_TARGETS, TARGET_TOKENS, 2 * KEY_VALUE_HEADS * HEAD_SIZE))
    return value_rows.astype(jnp.bfloat16)


def draw_target_queries(key, part):
    value_rows = starting_values(jax.random.fold_in(key, 23), (PART_TARGETS, TARGET_TOKENS, QUERY_HEADS * HEAD_SIZE))
    return value_rows.astype(jnp.bfloat16)


def draw_candidate_states(key, part):
    value_rows = starting_values(jax.random.fold_in(key, 24), (CANDIDATE_PAIRS, SOURCE_TOKENS, 2 * KEY_VALUE_HEADS * HEAD_SIZE))
    return value_rows.astype(jnp.bfloat16)


def draw_candidate_row(key, part):
    blocks = PART_TARGETS // TGT_DEV
    block_keys = jax.random.split(jax.random.fold_in(key, 31), blocks)
    orders = jax.vmap(lambda block_key: jax.random.permutation(block_key, CAND_DEV))(block_keys)
    return orders.reshape(PART_TARGETS, SLOTS).astype(jnp.int32)


def touch_ends(array, key, smallest, high):
    longest = array.shape.index(max(array.shape))
    spots = []
    for shift in (0, 1):
        where = [jax.random.randint(jax.random.fold_in(key, axis), (), 0, length) for axis, length in enumerate(array.shape)]
        where[longest] = (where[longest] + shift) % array.shape[longest]
        spots.append(tuple(where))
    return array.at[spots[0]].set(smallest).at[spots[1]].set(high)


def bell_draw(key, extent, scale, bound, held_as=jnp.bfloat16):
    return jnp.clip(scale * jax.random.normal(key, extent, jnp.float32), -bound, bound).astype(held_as)


def setup_inputs(seed: int = 0, part: int = 0) -> dict:
    keys = jax.random.split(jax.random.key(seed), 10)
    own_keys = jax.random.split(jax.random.fold_in(keys[9], part), 10)
    return {
        "candidate_queries": draw_candidate_queries(jax.random.fold_in(jax.random.fold_in(keys[9], part), 71), part),
        "target_states": draw_target_states(jax.random.fold_in(jax.random.fold_in(keys[9], part), 71), part),
        "target_queries": draw_target_queries(jax.random.fold_in(jax.random.fold_in(keys[9], part), 71), part),
        "candidate_states": draw_candidate_states(jax.random.fold_in(jax.random.fold_in(keys[9], part), 71), part),
        "target_length": touch_ends(jax.random.randint(own_keys[4], (PART_TARGETS,), 2, TARGET_TOKENS + 1), jax.random.fold_in(own_keys[4], 1), 2, TARGET_TOKENS).astype(jnp.int32),
        "candidate_length": touch_ends(jax.random.randint(own_keys[5], (PART_TARGETS, SLOTS), 2, SOURCE_TOKENS + 1), jax.random.fold_in(own_keys[5], 1), 2, SOURCE_TOKENS).astype(jnp.int32),
        "candidate_row": draw_candidate_row(jax.random.fold_in(jax.random.fold_in(keys[9], part), 71), part),
        "direct_readout": bell_draw(keys[7], (QW,), HEAD_SIZE ** -0.5, 0.5),
        "channel_readout": bell_draw(keys[8], (QW,), HEAD_SIZE ** -0.5, 0.5),
    }


masked_score = -1e+30

def attend_one(query_rows, hidden_states, length):
    count_of_rows = query_rows.shape[0]
    length_of_keys = hidden_states.shape[0]
    grouped_heads = query_rows.reshape(count_of_rows, KEY_VALUE_HEADS, QUERY_HEADS // KEY_VALUE_HEADS, HEAD_SIZE).astype(jnp.float32)
    split_halves = hidden_states.reshape(length_of_keys, 2, KEY_VALUE_HEADS, HEAD_SIZE).astype(jnp.float32)
    scores = jnp.einsum('rgqd,kgd->gqrk', grouped_heads, split_halves[:, 0]) * (1.0 / math.sqrt(HEAD_SIZE))
    usable = jnp.arange(length_of_keys, dtype=jnp.int32) < length
    scores = jnp.where(usable, scores, masked_score)
    highest = lax.optimization_barrier(jnp.max(scores, axis=-1, keepdims=True))
    weights = jnp.exp(scores - highest)
    rounded = lax.optimization_barrier((weights / lax.optimization_barrier(jnp.sum(weights, axis=-1, keepdims=True))).astype(jnp.bfloat16))
    mixture = jnp.einsum('gqrk,kgd->rgqd', rounded.astype(jnp.float32), split_halves[:, 1])
    return mixture.astype(jnp.bfloat16).reshape(count_of_rows, QUERY_HEADS * HEAD_SIZE)

def pooled(mixture, readout, length):
    tokens = jnp.dot(mixture, readout, preferred_element_type=jnp.float32)
    usable = jnp.arange(tokens.shape[0], dtype=jnp.int32) < length
    return jnp.sum(jnp.where(usable, tokens, 0.0)) / length.astype(jnp.float32)

def reference(candidate_queries, target_states, target_queries, candidate_states, target_length, candidate_length, candidate_row, direct_readout, channel_readout):
    target_index = jnp.arange(PART_TARGETS, dtype=jnp.int32)
    stored = candidate_row // PEER_ROWS * CAND_DEV + (target_index // TGT_DEV)[:, None] * PEER_ROWS + candidate_row % PEER_ROWS

    def score_target(index):
        lengths = candidate_length[index]
        own_length = target_length[index]

        def per_slot(slot):
            direct_mix = attend_one(candidate_queries[index, slot], target_states[index], own_length)
            direct = pooled(direct_mix, direct_readout, lengths[slot])
            hidden_states = candidate_states[stored[index, slot]]
            channel_mix = attend_one(target_queries[index], hidden_states, lengths[slot])
            channel = pooled(channel_mix, channel_readout, own_length)
            return direct + channel
        return jax.vmap(per_slot)(jnp.arange(SLOTS, dtype=jnp.int32))
    combined = lax.map(score_target, target_index)
    flat_rows = stored.reshape(CANDIDATE_PAIRS)
    return jnp.zeros((CANDIDATE_PAIRS,), jnp.float32).at[flat_rows].set(combined.reshape(CANDIDATE_PAIRS))
```

```python
import functools
import math

import jax
import jax.numpy as jnp
from jax import lax
from jax.experimental import pallas as pl
from jax.experimental.pallas import tpu as pltpu
from jax.sharding import PartitionSpec as P

HEAD_SIZE = 128
AXIS = "dp"
MESH = pl.DeviceIdType.MESH
EARLY = 2
masked_score = -1e30


def dot_nt(a, b):
    return lax.dot_general(
        a, b, (((1,), (1,)), ((), ())), preferred_element_type=jnp.float32
    )


class Peers:
    def __init__(self, me, n):
        assert n >= 4 and n & (n - 1) == 0
        m = n // 4
        self.me, self.n, self.m = me, n, m
        self.quarter = lax.div(me, m)
        low = 1 - 2 * lax.rem(self.quarter, 2)
        high = 1 - 2 * lax.div(self.quarter, 2)
        self.outer = lax.rem(self.quarter + lax.div(self.quarter, 2), 2) == 0
        one, two = low * m, high * (2 * m)
        self.one, self.two, self.three = me + one, me + two, me + one + two
        self.far = lax.select(self.outer, self.three, self.two)
        self.near = lax.select(self.outer, self.two, self.three)
        steps, bit = [0], 1
        while bit < m:
            step = (1 - 2 * lax.rem(lax.div(me, bit), 2)) * bit
            steps = steps + [s + step for s in steps]
            bit *= 2
        self.steps = steps

    def inside(self):
        return [self.me + s for s in self.steps[1:]]

    def at(self, base):
        return [base + s for s in self.steps]

    def arrival(self, i):
        m = self.m
        late = i - (2 * m - 1)
        j = lax.select(i < m - 1, i + 1, lax.select(late < 0, i - (m - 1), lax.div(late, 2)))
        base = lax.select(
            i < m - 1, self.me,
            lax.select(late < 0, self.far, lax.select(lax.rem(late, 2) == 0, self.one, self.near)),
        )
        peer, bit = base, 1
        while bit < m:
            step = (1 - 2 * lax.rem(lax.div(self.me, bit), 2)) * bit
            peer = peer + step * lax.rem(lax.div(j, bit), 2)
            bit *= 2
        return peer


def ratio(scores, values, keys_left):
    keys = lax.broadcasted_iota(jnp.int32, scores.shape, 0)
    scores = jnp.where(keys < keys_left, scores, masked_score)
    highest = jnp.max(scores, axis=0, keepdims=True)
    factor = math.log2(math.e) / math.sqrt(HEAD_SIZE)
    weights = jnp.exp2((scores - highest) * factor)
    return jnp.sum(weights * values, axis=0, keepdims=True) / jnp.sum(
        weights, axis=0, keepdims=True
    )


def kernel(
    n, dims,
    stored_in, sources_in, lengths_in, direct_in, channel_in, cq, ts, tq, cs,
    out,
    stored, sources, lengths, direct_r, channel_r,
    cq_buf, ts_buf, tq_buf, v_buf, k_buf, u_out, u_buf, spread, ud, rd, sel, dsum, r_out, r_buf,
    in_sem, cq_sem, ks, kr, us, ur, rs, rr, ready,
):
    T, S, I, J, H, G = dims
    C = T * S
    rpp = C // n
    hg = H // G
    D = HEAD_SIZE
    me = lax.axis_index(AXIS)

    loads = [
        pltpu.make_async_copy(cs.at[:, :, :, pl.ds(G * D, G * D)], v_buf, in_sem.at[0]),
        pltpu.make_async_copy(
            cs.at[me, :, :, pl.ds(0, G * D)], k_buf.at[me], in_sem.at[1]
        ),
        pltpu.make_async_copy(ts, ts_buf, in_sem.at[2]),
        pltpu.make_async_copy(tq, tq_buf, in_sem.at[3]),
        pltpu.make_async_copy(channel_in, channel_r, in_sem.at[4]),
        pltpu.make_async_copy(direct_in, direct_r, in_sem.at[5]),
        pltpu.make_async_copy(stored_in, stored, in_sem.at[6]),
        pltpu.make_async_copy(sources_in, sources, in_sem.at[7]),
        pltpu.make_async_copy(lengths_in, lengths, in_sem.at[8]),
    ]
    def cq_copy(t):
        return pltpu.make_async_copy(cq.at[t], cq_buf.at[t], cq_sem.at[t])

    barrier = pltpu.get_barrier_semaphore()
    peers = Peers(me, n)
    m = n // 4
    last = peers.quarter == 3

    def say(peer, semaphore):
        pl.semaphore_signal(
            semaphore, inc=1, device_id={AXIS: peer}, device_id_type=MESH
        )

    for peer in peers.inside():
        say(peer, barrier)
    cross = peers.at(peers.two) + peers.at(peers.three)
    for peer in cross + peers.at(peers.one):
        @pl.when(jnp.logical_or(jnp.logical_not(last), lax.div(peer, m) == 3))
        def _(peer=peer):
            say(peer, barrier)

    for load in loads[4:]:
        load.start()
    loads[0].start()
    loads[2].start()
    cq_copy(0).start()

    def k_copy(p, slot):
        return pltpu.make_async_remote_copy(
            src_ref=cs.at[p, :, :, pl.ds(0, G * D)],
            dst_ref=k_buf.at[slot], send_sem=ks.at[p], recv_sem=kr.at[slot],
            device_id={AXIS: p}, device_id_type=MESH,
        )

    def u_copy(p, slot):
        return pltpu.make_async_remote_copy(
            src_ref=u_out.at[p], dst_ref=u_buf.at[slot], send_sem=us.at[p],
            recv_sem=ur.at[slot], device_id={AXIS: p}, device_id_type=MESH,
        )

    def r_copy(p, slot):
        return pltpu.make_async_remote_copy(
            src_ref=r_out.at[p], dst_ref=r_buf.at[slot], send_sem=rs.at[p],
            recv_sem=rr.at[slot], device_id={AXIS: p}, device_id_type=MESH,
        )

    @pl.when(last)
    def _():
        pl.semaphore_wait(barrier, n - 1)
        for peer in cross + peers.at(peers.one):
            say(peer, ready)

    @pl.when(jnp.logical_not(last))
    def _():
        pl.semaphore_wait(barrier, n - 1 - m)

    inner = lax.div(peers.quarter, 2) == 0
    first = lax.select(inner, lax.select(peers.outer, peers.near, peers.near), peers.far)
    first = peers.at(first)[: min(EARLY, m)]
    second = peers.at(peers.far)
    third = peers.at(peers.near)
    for peer in first:
        k_copy(peer, me).start()
    loads[1].start()
    for t in range(1, T):
        cq_copy(t).start()
    loads[3].start()

    wide = u_out.shape[2]
    head_id = lax.broadcasted_iota(jnp.int32, (H, D), 0)
    rows_r = jnp.zeros((H, D), jnp.float32)
    loads[4].wait()
    for h in range(H):
        row = channel_r[h * D : (h + 1) * D].astype(jnp.float32).reshape(1, D)
        rows_r = jnp.where(head_id == h, row, rows_r)
    rows_r = jnp.concatenate([rows_r.astype(jnp.bfloat16)] * (wide // H), axis=0)
    row_id = lax.broadcasted_iota(jnp.int32, (wide, D), 0)
    loads[0].wait()
    u = None
    for r in range(rpp):
        for g in range(G):
            weights = jnp.where(
                row_id // hg == r * G + g, rows_r, jnp.zeros_like(rows_r)
            )
            values = v_buf[:, r, :, g * D : (g + 1) * D]
            values = values.reshape(n * I, D)
            part = dot_nt(values, weights)
            u = part if u is None else u + part
    u_out[...] = u.astype(jnp.bfloat16).reshape(n, I, wide)

    lane = lax.broadcasted_iota(jnp.int32, (wide, hg * J), 1)
    head = lax.broadcasted_iota(jnp.int32, (wide, hg * J), 0)
    for r in range(rpp):
        for g in range(G):
            hit = head == lane // J + (r * H + g * hg)
            sel[r * G + g] = jnp.where(hit, 1.0, 0.0).astype(jnp.bfloat16)

    @pl.when(jnp.logical_not(last))
    def _():
        pl.semaphore_wait(ready, m)

    for peer in second + third + peers.inside() + peers.at(peers.one):
        u_copy(peer, me).start()
    early = len(first)
    for k, peer in enumerate(second):
        if k < early:
            @pl.when(inner)
            def _(peer=peer):
                k_copy(peer, me).start()
        else:
            k_copy(peer, me).start()
    for k, peer in enumerate(third):
        if k < early:
            @pl.when(jnp.logical_not(inner))
            def _(peer=peer):
                k_copy(peer, me).start()
        else:
            k_copy(peer, me).start()
    for peer in peers.inside() + peers.at(peers.one):
        k_copy(peer, me).start()

    rows = S * I
    slot = lax.broadcasted_iota(jnp.int32, (1, rows), 1) // I
    for load in loads[5:]:
        load.wait()
    for t in range(T):
        held = jnp.zeros((1, rows), jnp.int32)
        count = jnp.zeros((1, rows), jnp.int32)
        for c in range(S):
            held = jnp.where(slot == c, stored[t, c], held)
            count = jnp.where(slot == c, sources[t, c], count)
        spread[0, t] = held
        spread[1, t] = count
        spread[2, t] = (count * (J + 1) + lengths[t]) * T + t

    loads[2].wait()
    for g in range(G):
        states = ts_buf[:, :, (G + g) * D : (G + g + 1) * D].reshape(T * J, D)
        for q in range(hg):
            h = g * hg + q
            rd[q * rows : (q + 1) * rows, :] = jnp.broadcast_to(
                direct_r[h * D : (h + 1) * D].astype(jnp.float32).reshape(1, D), (rows, D)
            ).astype(jnp.bfloat16)
        ud[g] = dot_nt(states, rd[...])

    token = lax.rem(lax.broadcasted_iota(jnp.int32, (1, rows), 1), I)

    def direct(t, carry):
        cq_copy(t).wait()
        total = jnp.zeros((1, hg * rows), jnp.float32)
        for g in range(G):
            queries = jnp.concatenate(
                [
                    cq_buf[t, :, (g * hg + q) * D : (g * hg + q + 1) * D]
                    for q in range(hg)
                ],
                axis=0,
            )
            scores = dot_nt(ts_buf[t, :, g * D : (g + 1) * D], queries)
            values = ud[g, pl.ds(pl.multiple_of(t * J, J), J), :]
            total = total + ratio(scores, values, lengths[t])
        tokens = total[:, 0:rows]
        for q in range(1, hg):
            tokens = tokens + total[:, q * rows : (q + 1) * rows]
        count = spread[1, t]
        dsum[t] = jnp.where(token < count, tokens, 0.0) / count.astype(jnp.float32)
        return carry

    lax.fori_loop(0, T, direct, 0)

    loads[3].wait()
    lanes = out.shape[1]
    place = lax.broadcasted_iota(jnp.int32, (1, lanes), 1)
    position = lax.rem(lax.broadcasted_iota(jnp.int32, (1, hg * J), 1), J)
    direct_sums = dsum[...]
    owners = spread[0]
    codes = spread[2]

    def lookup(p):
        return [
            jnp.max(jnp.where(owners == p * rpp + r, codes, 0)) for r in range(rpp)
        ]

    def block(p, found):
        result = jnp.zeros((1, lanes), jnp.float32)
        sent = u_buf[p]
        for r in range(rpp):
            v = p * rpp + r
            t = lax.rem(found[r], T)
            target_count = lax.rem(found[r] // T, J + 1)
            source_count = found[r] // (T * (J + 1))
            total = jnp.zeros((1, hg * J), jnp.float32)
            for g in range(G):
                queries = jnp.concatenate(
                    [
                        tq_buf[t, :, (g * hg + q) * D : (g * hg + q + 1) * D]
                        for q in range(hg)
                    ],
                    axis=0,
                )
                scores = dot_nt(k_buf[p, r, :, g * D : (g + 1) * D], queries)
                values = jnp.dot(
                    sent, sel[r * G + g], preferred_element_type=jnp.float32
                )
                total = total + ratio(scores, values, source_count)
            kept = jnp.where(position < target_count, total, 0.0)
            channel = jnp.sum(kept, axis=1, keepdims=True)
            channel = channel / target_count.astype(jnp.float32)
            own = jnp.where(owners == v, direct_sums, 0.0)
            own = jnp.sum(jnp.sum(own, axis=0), axis=1, keepdims=True)
            result = result + jnp.where(place == me * rpp + r, own + channel, 0.0)
        return result

    u_buf[me] = u_out[me]
    loads[1].wait()
    r_buf[me] = block(me, lookup(me))

    def channel_step(i, carry):
        p = peers.arrival(i)
        found = lookup(p)
        k_copy(p, p).wait_recv()
        u_copy(p, p).wait_recv()
        r_out[p] = block(p, found)
        r_copy(p, me).start()
        return carry

    lax.fori_loop(0, n - 1, channel_step, 0)

    def finish(i, carry):
        p = peers.arrival(i)
        r_copy(p, p).wait_recv()
        k_copy(p, p).wait_send()
        u_copy(p, p).wait_send()
        r_copy(p, p).wait_send()
        return carry

    lax.fori_loop(0, n - 1, finish, 0)
    out[...] = jnp.sum(r_buf[...], axis=0)


def on_device(
    n,
    candidate_queries,
    target_states,
    target_queries,
    candidate_states,
    target_length,
    candidate_length,
    candidate_row,
    direct_readout,
    channel_readout,
):
    T, S, I, QW = candidate_queries.shape
    J = target_states.shape[1]
    H = QW // HEAD_SIZE
    G = target_states.shape[2] // (2 * HEAD_SIZE)
    C = T * S
    rpp = C // n
    hg = H // G
    wide = max(128, rpp * H)
    lanes = -(-C // 128) * 128
    bf, f32 = jnp.bfloat16, jnp.float32
    vmem, smem = pltpu.VMEM, pltpu.SMEM
    anywhere = pl.BlockSpec(memory_space=pl.ANY)
    dma = pltpu.SemaphoreType.DMA
    found = pl.pallas_call(
        functools.partial(kernel, n, (T, S, I, J, H, G)),
        out_shape=jax.ShapeDtypeStruct((1, lanes), f32),
        in_specs=[
            anywhere, anywhere, anywhere, anywhere, anywhere,
            anywhere, anywhere, anywhere, anywhere,
        ],
        out_specs=pl.BlockSpec(memory_space=vmem),
        scratch_shapes=[
            smem((T, S), jnp.int32),
            smem((T, S), jnp.int32),
            smem((T,), jnp.int32),
            vmem((QW,), bf),
            vmem((QW,), bf),
            vmem((T, S * I, QW), bf),
            vmem(target_states.shape, bf),
            vmem(target_queries.shape, bf),
            vmem((n, rpp, I, G * HEAD_SIZE), bf),
            vmem((n, rpp, I, G * HEAD_SIZE), bf),
            vmem((n, I, wide), bf),
            vmem((n, I, wide), bf),
            vmem((3, T, 1, S * I), jnp.int32),
            vmem((G, T * J, hg * S * I), f32),
            vmem((hg * S * I, HEAD_SIZE), bf),
            vmem((rpp * G, wide, hg * J), bf),
            vmem((T, 1, S * I), f32),
            vmem((n, 1, lanes), f32),
            vmem((n, 1, lanes), f32),
            dma((9,)), dma((T,)),
            dma((n,)), dma((n,)), dma((n,)), dma((n,)), dma((n,)), dma((n,)),
            pltpu.SemaphoreType.REGULAR,
        ],
        compiler_params=pltpu.CompilerParams(
            collective_id=0, has_side_effects=True, vmem_limit_bytes=60 << 20
        ),
    )(
        candidate_row, candidate_length, target_length,
        direct_readout, channel_readout,
        candidate_queries.reshape(T, S * I, QW),
        target_states, target_queries,
        candidate_states.reshape(n, rpp, I, 2 * G * HEAD_SIZE),
    )
    return found[0, :C]


def solution(mesh):
    in_specs = (
        P(("group", "dp"), None, None, None),
        P(("group", "dp"), None, None),
        P(("group", "dp"), None, None),
        P(("group", "dp"), None, None),
        P(("group", "dp")),
        P(("group", "dp"), None),
        P(("group", "dp"), None),
        P(),
        P(),
    )
    return jax.shard_map(
        functools.partial(on_device, mesh.shape[AXIS]),
        mesh=mesh, in_specs=in_specs, out_specs=P(("group", "dp")), check_vma=False,
    )
```

```python
import functools
import math

import jax
import jax.numpy as jnp
from jax import lax
from jax.experimental import pallas as pl
from jax.experimental.pallas import tpu as pltpu
from jax.sharding import PartitionSpec as P

HEAD_SIZE = 128
AXIS = "dp"
MESH = pl.DeviceIdType.MESH
EARLY = 2
HELD = 2
masked_score = -1e30


def dot_nt(a, b):
    return lax.dot_general(
        a, b, (((1,), (1,)), ((), ())), preferred_element_type=jnp.float32
    )


class Peers:
    def __init__(self, me, n):
        assert n >= 4 and n & (n - 1) == 0
        m = n // 4
        self.me, self.n, self.m = me, n, m
        self.quarter = lax.div(me, m)
        low = 1 - 2 * lax.rem(self.quarter, 2)
        high = 1 - 2 * lax.div(self.quarter, 2)
        self.outer = lax.rem(self.quarter + lax.div(self.quarter, 2), 2) == 0
        one, two = low * m, high * (2 * m)
        self.one, self.two, self.three = me + one, me + two, me + one + two
        self.far = lax.select(self.outer, self.three, self.two)
        self.near = lax.select(self.outer, self.two, self.three)
        steps, bit = [0], 1
        while bit < m:
            step = (1 - 2 * lax.rem(lax.div(me, bit), 2)) * bit
            steps = steps + [s + step for s in steps]
            bit *= 2
        self.steps = steps

    def inside(self):
        return [self.me + s for s in self.steps[1:]]

    def at(self, base):
        return [base + s for s in self.steps]

    def arrival(self, i):
        m = self.m
        i = i - (m - 1)
        early = lax.select(self.outer, 0, min(EARLY, m // 2))
        late = i - early
        inside = i < 0
        near = jnp.logical_or(i < early, i >= 2 * m + early)
        j = lax.select(i < early, i, i - 2 * m)
        j = lax.select(near, m - 1 - j, lax.rem(late + m, m))
        j = lax.select(inside, i + m, j)
        base = lax.select(late < m, self.far, self.one)
        base = lax.select(near, self.near, base)
        base = lax.select(inside, self.me, base)
        peer, bit = base, 1
        while bit < m:
            step = (1 - 2 * lax.rem(lax.div(self.me, bit), 2)) * bit
            peer = peer + step * lax.rem(lax.div(j, bit), 2)
            bit *= 2
        return peer


def ratio(scores, values, keys_left):
    keys = lax.broadcasted_iota(jnp.int32, scores.shape, 0)
    scores = jnp.where(keys < keys_left, scores, masked_score)
    highest = jnp.max(scores, axis=0, keepdims=True)
    factor = math.log2(math.e) / math.sqrt(HEAD_SIZE)
    weights = jnp.exp2((scores - highest) * factor)
    return jnp.sum(weights * values, axis=0, keepdims=True) / jnp.sum(
        weights, axis=0, keepdims=True
    )


def kernel(
    n, dims,
    stored_in, sources_in, lengths_in, direct_in, channel_in, cq, ts, tq, cs,
    out,
    stored, sources, lengths, table, direct_r, channel_r,
    cq_buf, ts_buf, tq_buf, v_buf, k_buf, u_out, u_buf, spread, owners, ud, rd, sel, score, owned, owned_count, dsum, owns, r_out, r_buf,
    in_sem, cq_sem, ks, kr, us, ur, rs, rr, ready,
):
    T, S, I, J, H, G = dims
    C = T * S
    rpp = C // n
    hg = H // G
    D = HEAD_SIZE
    me = lax.axis_index(AXIS)

    loads = [
        pltpu.make_async_copy(cs.at[:, :, :, pl.ds(G * D, G * D)], v_buf, in_sem.at[0]),
        pltpu.make_async_copy(
            cs.at[me, :, :, pl.ds(0, G * D)], k_buf.at[me], in_sem.at[1]
        ),
        pltpu.make_async_copy(ts, ts_buf, in_sem.at[2]),
        pltpu.make_async_copy(tq, tq_buf, in_sem.at[3]),
        pltpu.make_async_copy(channel_in, channel_r, in_sem.at[4]),
        pltpu.make_async_copy(direct_in, direct_r, in_sem.at[5]),
        pltpu.make_async_copy(stored_in, stored, in_sem.at[6]),
        pltpu.make_async_copy(sources_in, sources, in_sem.at[7]),
        pltpu.make_async_copy(lengths_in, lengths, in_sem.at[8]),
        pltpu.make_async_copy(stored_in, owned, in_sem.at[9]),
        pltpu.make_async_copy(sources_in, owned_count, in_sem.at[10]),
    ]
    def cq_copy(t):
        return pltpu.make_async_copy(cq.at[t], cq_buf.at[t], cq_sem.at[t])

    barrier = pltpu.get_barrier_semaphore()
    peers = Peers(me, n)
    m = n // 4
    last = peers.quarter == 3

    def say(peer, semaphore):
        pl.semaphore_signal(
            semaphore, inc=1, device_id={AXIS: peer}, device_id_type=MESH
        )

    for peer in peers.inside():
        say(peer, barrier)
    cross = peers.at(peers.two) + peers.at(peers.three)

    @pl.when(jnp.logical_not(last))
    def _():
        for peer in cross + peers.at(peers.one):
            say(peer, barrier)

    for load in loads[4:]:
        load.start()
    loads[0].start()
    loads[2].start()
    cq_copy(0).start()

    def k_copy(p, slot):
        return pltpu.make_async_remote_copy(
            src_ref=cs.at[p, :, :, pl.ds(0, G * D)],
            dst_ref=k_buf.at[slot], send_sem=ks, recv_sem=kr.at[slot],
            device_id={AXIS: p}, device_id_type=MESH,
        )

    def u_copy(p, slot):
        return pltpu.make_async_remote_copy(
            src_ref=u_out.at[p], dst_ref=u_buf.at[slot], send_sem=us,
            recv_sem=ur.at[slot], device_id={AXIS: p}, device_id_type=MESH,
        )

    def r_copy(p, slot):
        return pltpu.make_async_remote_copy(
            src_ref=r_out.at[p], dst_ref=r_buf.at[slot], send_sem=rs,
            recv_sem=rr, device_id={AXIS: p}, device_id_type=MESH,
        )

    @pl.when(last)
    def _():
        pl.semaphore_wait(barrier, n - 1)
        for peer in cross + peers.at(peers.one):
            say(peer, ready)

    @pl.when(jnp.logical_not(last))
    def _():
        pl.semaphore_wait(barrier, n - 1 - m)

    early = min(EARLY, m // 2)
    far = peers.at(peers.far)
    near = peers.at(peers.near)[::-1]
    for peer in near[:early]:
        k_copy(peer, me).start()
    loads[1].start()
    for t in range(1, T):
        cq_copy(t).start()
    loads[3].start()

    wide = u_out.shape[2]
    head_id = lax.broadcasted_iota(jnp.int32, (H, D), 0)
    rows_r = jnp.zeros((H, D), jnp.float32)
    loads[4].wait()
    for h in range(H):
        row = channel_r[h * D : (h + 1) * D].astype(jnp.float32).reshape(1, D)
        rows_r = jnp.where(head_id == h, row, rows_r)
    rows_r = jnp.concatenate([rows_r.astype(jnp.bfloat16)] * (wide // H), axis=0)
    row_id = lax.broadcasted_iota(jnp.int32, (wide, D), 0)
    loads[0].wait()
    u = None
    for r in range(rpp):
        for g in range(G):
            weights = jnp.where(
                row_id // hg == r * G + g, rows_r, jnp.zeros_like(rows_r)
            )
            values = v_buf[:, r, :, g * D : (g + 1) * D]
            values = values.reshape(n * I, D)
            part = dot_nt(values, weights)
            u = part if u is None else u + part
    turn = lax.rem(lax.broadcasted_iota(jnp.int32, u.shape, 1), hg)
    for q in range(1, hg):
        error = u - u.astype(jnp.bfloat16).astype(jnp.float32)
        u = jnp.where(turn == q, u + pltpu.roll(error, 1, 1), u)
    u_out[...] = u.astype(jnp.bfloat16).reshape(n, I, wide)

    lane = lax.broadcasted_iota(jnp.int32, (hg * J, wide), 1)
    head = lax.broadcasted_iota(jnp.int32, (hg * J, wide), 0) // J
    sel[...] = jnp.where(lax.rem(lane, hg) == head, 1.0, 0.0).astype(jnp.bfloat16)

    @pl.when(jnp.logical_not(last))
    def _():
        pl.semaphore_wait(ready, m)

    other = peers.inside() + peers.at(peers.one)
    for peer in near[:early] + far + near[early:] + other:
        u_copy(peer, me).start()
    back = near[max(early, m - HELD) :]
    for peer in far + near[early : max(early, m - HELD)] + other:
        k_copy(peer, me).start()

    for peer in back:
        k_copy(peer, me).start()

    rows = S * I
    slot = lax.broadcasted_iota(jnp.int32, (1, rows), 1) // I
    for load in loads[5:]:
        load.wait()
    for t in range(T):
        held = jnp.zeros((1, rows), jnp.int32)
        count = jnp.zeros((1, rows), jnp.int32)
        for c in range(S):
            held = jnp.where(slot == c, stored[t, c], held)
            count = jnp.where(slot == c, sources[t, c], count)
        owners[t : t + 1, :] = held
        spread[t : t + 1, :] = count

    loads[2].wait()
    for g in range(G):
        states = ts_buf[:, :, (G + g) * D : (G + g + 1) * D].reshape(T * J, D)
        for q in range(hg):
            h = g * hg + q
            rd[q * rows : (q + 1) * rows, :] = jnp.broadcast_to(
                direct_r[h * D : (h + 1) * D].astype(jnp.float32).reshape(1, D), (rows, D)
            ).astype(jnp.bfloat16)
        ud[g] = dot_nt(states, rd[...])

    held = owned[...]
    target = lax.broadcasted_iota(jnp.int32, (T, S), 0)
    target_counts = jnp.zeros((T, S), jnp.int32)
    for t in range(T):
        target_counts = jnp.where(target == t, lengths[t], target_counts)
    codes = (owned_count[...] * (J + 1) + target_counts) * T + target
    for v in range(C):
        table[v] = jnp.max(jnp.where(held == v, codes, 0))

    token = lax.rem(lax.broadcasted_iota(jnp.int32, (1, rows), 1), I)

    def direct(t, carry):
        cq_copy(t).wait()
        total = jnp.zeros((1, hg * rows), jnp.float32)
        for g in range(G):
            queries = jnp.concatenate(
                [
                    cq_buf[t, :, (g * hg + q) * D : (g * hg + q + 1) * D]
                    for q in range(hg)
                ],
                axis=0,
            )
            scores = dot_nt(ts_buf[t, :, g * D : (g + 1) * D], queries)
            values = ud[g, pl.ds(pl.multiple_of(t * J, J), J), :]
            total = total + ratio(scores, values, lengths[t])
        tokens = total[:, 0:rows]
        for q in range(1, hg):
            tokens = tokens + total[:, q * rows : (q + 1) * rows]
        count = spread[pl.ds(t, 1), :]
        dsum[pl.ds(t, 1), :] = jnp.where(token < count, tokens, 0.0) / count.astype(jnp.float32)
        return carry

    lax.fori_loop(0, T, direct, 0)

    loads[3].wait()
    lanes = out.shape[1]
    direct_sums = dsum[...]
    owner = owners[...]
    rows_of = wide // rpp
    spot = lax.broadcasted_iota(jnp.int32, (T, wide), 1)
    for p in range(n):
        own = jnp.zeros((T, wide), jnp.float32)
        for r in range(rpp):
            part = jnp.where(owner == p * rpp + r, direct_sums, 0.0)
            part = jnp.sum(part, axis=1, keepdims=True)
            own = jnp.where(spot == r * rows_of, part, own)
        owns[p] = own
    RG = rpp * G
    key = lax.broadcasted_iota(jnp.int32, (I, hg * J), 0)
    row_of = lax.broadcasted_iota(jnp.int32, (RG, hg * J), 0) // G
    position = lax.rem(lax.broadcasted_iota(jnp.int32, (RG, hg * J), 1), J)
    row_of_sum = lax.broadcasted_iota(jnp.int32, (RG, wide), 0)
    own_lanes = lax.broadcasted_iota(jnp.int32, (RG, wide), 1) // hg == row_of_sum
    factor = math.log2(math.e) / math.sqrt(D)

    def lookup(p):
        return [table[p * rpp + r] for r in range(rpp)]

    def block(p, found):
        limits = jnp.zeros((RG, hg * J), jnp.int32)
        divisors = jnp.ones((RG, wide), jnp.float32)
        for r in range(rpp):
            t = lax.rem(found[r], T)
            target_count = lax.rem(found[r] // T, J + 1)
            source_count = found[r] // (T * (J + 1))
            limits = jnp.where(row_of == r, target_count, limits)
            divisors = jnp.where(
                row_of_sum // G == r, target_count.astype(jnp.float32), divisors
            )
            usable = key < source_count
            for g in range(G):
                queries = jnp.concatenate(
                    [
                        tq_buf[t, :, (g * hg + q) * D : (g * hg + q + 1) * D]
                        for q in range(hg)
                    ],
                    axis=0,
                )
                scores = dot_nt(k_buf[p, r, :, g * D : (g + 1) * D], queries)
                scores = jnp.where(usable, scores, masked_score)
                for c in range(0, hg * J, 128):
                    score[c // 128, pl.ds(r * G + g, I, stride=RG), :] = scores[:, c : c + 128]
        def at(k):
            return jnp.concatenate(
                [score[c, k * RG : (k + 1) * RG, :] for c in range(hg * J // 128)], axis=1
            )
        highest = at(0)
        for k in range(1, I):
            highest = jnp.maximum(highest, at(k))
        weights = [jnp.exp2((at(k) - highest) * factor) for k in range(I)]
        total = weights[0]
        for k in range(1, I):
            total = total + weights[k]
        scale = jnp.where(position < limits, 1.0 / total, 0.0)
        probs = jnp.concatenate(
            [(w * scale).astype(jnp.bfloat16) for w in weights], axis=0
        )
        sums = jnp.dot(probs, sel[...], preferred_element_type=jnp.float32)
        u = u_buf[p].astype(jnp.float32)
        mixed = sums[0:RG] * u[0:1]
        for k in range(1, I):
            mixed = mixed + sums[k * RG : (k + 1) * RG] * u[k : k + 1]
        mixed = jnp.where(own_lanes, mixed / divisors, 0.0)
        return jnp.sum(mixed, axis=0, keepdims=True) + jnp.sum(owns[p], axis=0, keepdims=True)

    u_buf[me] = u_out[me]
    loads[1].wait()
    r_buf[me] = block(me, lookup(me))

    def channel_step(i, carry):
        p = peers.arrival(i)
        found = lookup(p)
        k_copy(p, p).wait_recv()
        u_copy(p, p).wait_recv()
        r_out[p] = block(p, found)
        r_copy(p, me).start()

        return carry

    lax.fori_loop(0, n - 1, channel_step, 0)

    def settle(buffer, semaphore):
        rest = buffer.at[pl.ds(0, n - 1)]
        pltpu.make_async_copy(rest, rest, semaphore).wait()

    settle(r_buf, rr)
    settle(k_buf, ks)
    settle(u_buf, us)
    settle(r_buf, rs)
    sums = r_buf[...].reshape(n, wide)
    part = lax.broadcasted_iota(jnp.int32, (n, wide), 1) // rows_of
    place = lax.broadcasted_iota(jnp.int32, (n, lanes), 1)
    source = lax.broadcasted_iota(jnp.int32, (n, lanes), 0)
    result = jnp.zeros((n, lanes), jnp.float32)
    for r in range(rpp):
        value = jnp.sum(jnp.where(part == r, sums, 0.0), axis=1, keepdims=True)
        result = jnp.where(place == source * rpp + r, value, result)
    out[...] = jnp.sum(result, axis=0, keepdims=True)


def on_device(
    n,
    candidate_queries,
    target_states,
    target_queries,
    candidate_states,
    target_length,
    candidate_length,
    candidate_row,
    direct_readout,
    channel_readout,
):
    T, S, I, QW = candidate_queries.shape
    J = target_states.shape[1]
    H = QW // HEAD_SIZE
    G = target_states.shape[2] // (2 * HEAD_SIZE)
    C = T * S
    rpp = C // n
    hg = H // G
    wide = max(128, rpp * H)
    lanes = -(-C // 128) * 128
    bf, f32 = jnp.bfloat16, jnp.float32
    vmem, smem = pltpu.VMEM, pltpu.SMEM
    anywhere = pl.BlockSpec(memory_space=pl.ANY)
    dma = pltpu.SemaphoreType.DMA
    found = pl.pallas_call(
        functools.partial(kernel, n, (T, S, I, J, H, G)),
        out_shape=jax.ShapeDtypeStruct((1, lanes), f32),
        in_specs=[
            anywhere, anywhere, anywhere, anywhere, anywhere,
            anywhere, anywhere, anywhere, anywhere,
        ],
        out_specs=pl.BlockSpec(memory_space=vmem),
        scratch_shapes=[
            smem((T, S), jnp.int32),
            smem((T, S), jnp.int32),
            smem((T,), jnp.int32),
            smem((C,), jnp.int32),
            vmem((QW,), bf),
            vmem((QW,), bf),
            vmem((T, S * I, QW), bf),
            vmem(target_states.shape, bf),
            vmem(target_queries.shape, bf),
            vmem((n, rpp, I, G * HEAD_SIZE), bf),
            vmem((n, rpp, I, G * HEAD_SIZE), bf),
            vmem((n, I, wide), bf),
            vmem((n, I, wide), bf),
            vmem((T, S * I), jnp.int32),
            vmem((T, S * I), jnp.int32),
            vmem((G, T * J, hg * S * I), f32),
            vmem((hg * S * I, HEAD_SIZE), bf),
            vmem((hg * J, wide), bf),
            vmem((hg * J // 128, I * rpp * G, 128), f32),
            vmem((T, S), jnp.int32),
            vmem((T, S), jnp.int32),
            vmem((T, S * I), f32),
            vmem((n, T, wide), f32),
            vmem((n, 1, wide), f32),
            vmem((n, 1, wide), f32),
            dma((11,)), dma((T,)),
            dma, dma((n,)), dma, dma((n,)), dma, dma,
            pltpu.SemaphoreType.REGULAR,
        ],
        compiler_params=pltpu.CompilerParams(
            collective_id=0, has_side_effects=True, vmem_limit_bytes=60 << 20
        ),
    )(
        candidate_row, candidate_length, target_length,
        direct_readout, channel_readout,
        candidate_queries.reshape(T, S * I, QW),
        target_states, target_queries,
        candidate_states.reshape(n, rpp, I, 2 * G * HEAD_SIZE),
    )
    return found[0, :C]


def solution(mesh):
    in_specs = (
        P(("group", "dp"), None, None, None),
        P(("group", "dp"), None, None),
        P(("group", "dp"), None, None),
        P(("group", "dp"), None, None),
        P(("group", "dp")),
        P(("group", "dp"), None),
        P(("group", "dp"), None),
        P(),
        P(),
    )
    return jax.shard_map(
        functools.partial(on_device, mesh.shape[AXIS]),
        mesh=mesh, in_specs=in_specs, out_specs=P(("group", "dp")), check_vma=False,
    )
```

```python
import functools
import math

import jax
import jax.numpy as jnp
from jax import lax
from jax.experimental import pallas as pl
from jax.experimental.pallas import tpu as pltpu
from jax.sharding import PartitionSpec as P

HEAD_SIZE = 128
AXIS = "dp"
MESH = pl.DeviceIdType.MESH
EARLY = 2
HELD = 2
masked_score = -1e30


def dot_nt(a, b):
    return lax.dot_general(
        a, b, (((1,), (1,)), ((), ())), preferred_element_type=jnp.float32
    )


class Peers:
    def __init__(self, me, n):
        assert n >= 4 and n & (n - 1) == 0
        m = n // 4
        self.me, self.n, self.m = me, n, m
        self.quarter = lax.div(me, m)
        low = 1 - 2 * lax.rem(self.quarter, 2)
        high = 1 - 2 * lax.div(self.quarter, 2)
        self.outer = lax.rem(self.quarter + lax.div(self.quarter, 2), 2) == 0
        one, two = low * m, high * (2 * m)
        self.one, self.two, self.three = me + one, me + two, me + one + two
        self.far = lax.select(self.outer, self.three, self.two)
        self.near = lax.select(self.outer, self.two, self.three)
        steps, bit = [0], 1
        while bit < m:
            step = (1 - 2 * lax.rem(lax.div(me, bit), 2)) * bit
            steps = steps + [s + step for s in steps]
            bit *= 2
        self.steps = steps

    def inside(self):
        return [self.me + s for s in self.steps[1:]]

    def at(self, base):
        return [base + s for s in self.steps]

    def arrival(self, i):
        m = self.m
        i = i - (m - 1)
        early = lax.select(self.outer, 0, min(EARLY, m // 2))
        late = i - early
        part = lax.div(lax.max(late, 0), m)
        near = jnp.logical_or(late < 0, part == 2)
        one = part == lax.select(self.outer, 1, 0)
        j = lax.select(near, lax.select(late < 0, i, i - 2 * m), late - part * m)
        back = jnp.logical_not(jnp.logical_or(self.outer, jnp.logical_and(one, late >= 0)))
        j = lax.select(back, m - 1 - j, j)
        base = lax.select(one, self.one, self.far)
        base = lax.select(near, self.near, base)
        inside = i < 0
        base = lax.select(inside, self.me, base)
        j = lax.select(inside, i + m, j)
        peer, bit = base, 1
        while bit < m:
            step = (1 - 2 * lax.rem(lax.div(self.me, bit), 2)) * bit
            peer = peer + step * lax.rem(lax.div(j, bit), 2)
            bit *= 2
        return peer


def ratio(scores, values, keys_left):
    keys = lax.broadcasted_iota(jnp.int32, scores.shape, 0)
    scores = jnp.where(keys < keys_left, scores, masked_score)
    highest = jnp.max(scores, axis=0, keepdims=True)
    factor = math.log2(math.e) / math.sqrt(HEAD_SIZE)
    weights = jnp.exp2((scores - highest) * factor)
    return jnp.sum(weights * values, axis=0, keepdims=True) / jnp.sum(
        weights, axis=0, keepdims=True
    )


def kernel(
    n, dims,
    stored_in, sources_in, lengths_in, direct_in, channel_in, cq, ts, tq, cs,
    out,
    stored, sources, lengths, table, direct_r, channel_r,
    cq_buf, ts_buf, tq_buf, v_buf, k_buf, u_out, u_buf, spread, owners, ud, rd, sel, score, owned, owned_count, dsum, owns, r_out, r_buf,
    in_sem, cq_sem, ks, kr, us, ur, rs, rr, ready,
):
    T, S, I, J, H, G = dims
    C = T * S
    rpp = C // n
    hg = H // G
    D = HEAD_SIZE
    me = lax.axis_index(AXIS)

    loads = [
        pltpu.make_async_copy(cs.at[:, :, :, pl.ds(G * D, G * D)], v_buf, in_sem.at[0]),
        pltpu.make_async_copy(
            cs.at[me, :, :, pl.ds(0, G * D)], k_buf.at[me], in_sem.at[1]
        ),
        pltpu.make_async_copy(ts, ts_buf, in_sem.at[2]),
        pltpu.make_async_copy(tq, tq_buf, in_sem.at[3]),
        pltpu.make_async_copy(channel_in, channel_r, in_sem.at[4]),
        pltpu.make_async_copy(direct_in, direct_r, in_sem.at[5]),
        pltpu.make_async_copy(stored_in, stored, in_sem.at[6]),
        pltpu.make_async_copy(sources_in, sources, in_sem.at[7]),
        pltpu.make_async_copy(lengths_in, lengths, in_sem.at[8]),
        pltpu.make_async_copy(stored_in, owned, in_sem.at[9]),
        pltpu.make_async_copy(sources_in, owned_count, in_sem.at[10]),
    ]
    def cq_copy(t):
        return pltpu.make_async_copy(cq.at[t], cq_buf.at[t], cq_sem.at[t])

    barrier = pltpu.get_barrier_semaphore()
    peers = Peers(me, n)
    m = n // 4
    last = peers.quarter == 3

    def say(peer, semaphore):
        pl.semaphore_signal(
            semaphore, inc=1, device_id={AXIS: peer}, device_id_type=MESH
        )

    for peer in peers.inside():
        say(peer, barrier)
    cross = peers.at(peers.two) + peers.at(peers.three)

    @pl.when(jnp.logical_not(last))
    def _():
        for peer in cross + peers.at(peers.one):
            say(peer, barrier)

    for load in loads[4:]:
        load.start()
    loads[0].start()
    loads[2].start()
    cq_copy(0).start()

    def k_copy(p, slot):
        return pltpu.make_async_remote_copy(
            src_ref=cs.at[p, :, :, pl.ds(0, G * D)],
            dst_ref=k_buf.at[slot], send_sem=ks, recv_sem=kr.at[slot],
            device_id={AXIS: p}, device_id_type=MESH,
        )

    def u_copy(p, slot):
        return pltpu.make_async_remote_copy(
            src_ref=u_out.at[p], dst_ref=u_buf.at[slot], send_sem=us,
            recv_sem=ur.at[slot], device_id={AXIS: p}, device_id_type=MESH,
        )

    def r_copy(p, slot):
        return pltpu.make_async_remote_copy(
            src_ref=r_out.at[p], dst_ref=r_buf.at[slot], send_sem=rs,
            recv_sem=rr, device_id={AXIS: p}, device_id_type=MESH,
        )

    @pl.when(last)
    def _():
        pl.semaphore_wait(barrier, n - 1)
        for peer in cross + peers.at(peers.one):
            say(peer, ready)

    @pl.when(jnp.logical_not(last))
    def _():
        pl.semaphore_wait(barrier, n - 1 - m)

    early = min(EARLY, m // 2)
    far = peers.at(peers.far)
    near = peers.at(peers.near)[::-1]
    for peer in near[:early]:
        k_copy(peer, me).start()
    loads[1].start()
    for t in range(1, T):
        cq_copy(t).start()
    loads[3].start()

    wide = u_out.shape[2]
    head_id = lax.broadcasted_iota(jnp.int32, (H, D), 0)
    rows_r = jnp.zeros((H, D), jnp.float32)
    loads[4].wait()
    for h in range(H):
        row = channel_r[h * D : (h + 1) * D].astype(jnp.float32).reshape(1, D)
        rows_r = jnp.where(head_id == h, row, rows_r)
    rows_r = jnp.concatenate([rows_r.astype(jnp.bfloat16)] * (wide // H), axis=0)
    row_id = lax.broadcasted_iota(jnp.int32, (wide, D), 0)
    loads[0].wait()
    u = None
    for r in range(rpp):
        for g in range(G):
            weights = jnp.where(
                row_id // hg == r * G + g, rows_r, jnp.zeros_like(rows_r)
            )
            values = v_buf[:, r, :, g * D : (g + 1) * D]
            values = values.reshape(n * I, D)
            part = dot_nt(values, weights)
            u = part if u is None else u + part
    turn = lax.rem(lax.broadcasted_iota(jnp.int32, u.shape, 1), hg)
    for q in range(1, hg):
        error = u - u.astype(jnp.bfloat16).astype(jnp.float32)
        u = jnp.where(turn == q, u + pltpu.roll(error, 1, 1), u)
    u_out[...] = u.astype(jnp.bfloat16).reshape(n, I, wide)

    lane = lax.broadcasted_iota(jnp.int32, (hg * J, wide), 1)
    head = lax.broadcasted_iota(jnp.int32, (hg * J, wide), 0) // J
    sel[...] = jnp.where(lax.rem(lane, hg) == head, 1.0, 0.0).astype(jnp.bfloat16)

    @pl.when(jnp.logical_not(last))
    def _():
        pl.semaphore_wait(ready, m)

    other = peers.inside() + peers.at(peers.one)
    for peer in near[:early] + far + near[early:] + other:
        u_copy(peer, me).start()
    back = near[max(early, m - HELD) :]
    for peer in far + near[early : max(early, m - HELD)] + other:
        k_copy(peer, me).start()

    for peer in back:
        k_copy(peer, me).start()

    rows = S * I
    slot = lax.broadcasted_iota(jnp.int32, (1, rows), 1) // I
    for load in loads[5:]:
        load.wait()
    for t in range(T):
        held = jnp.zeros((1, rows), jnp.int32)
        count = jnp.zeros((1, rows), jnp.int32)
        for c in range(S):
            held = jnp.where(slot == c, stored[t, c], held)
            count = jnp.where(slot == c, sources[t, c], count)
        owners[t : t + 1, :] = held
        spread[t : t + 1, :] = count

    loads[2].wait()
    for g in range(G):
        states = ts_buf[:, :, (G + g) * D : (G + g + 1) * D].reshape(T * J, D)
        for q in range(hg):
            h = g * hg + q
            rd[q * rows : (q + 1) * rows, :] = jnp.broadcast_to(
                direct_r[h * D : (h + 1) * D].astype(jnp.float32).reshape(1, D), (rows, D)
            ).astype(jnp.bfloat16)
        ud[g] = dot_nt(states, rd[...])

    held = owned[...]
    target = lax.broadcasted_iota(jnp.int32, (T, S), 0)
    target_counts = jnp.zeros((T, S), jnp.int32)
    for t in range(T):
        target_counts = jnp.where(target == t, lengths[t], target_counts)
    codes = (owned_count[...] * (J + 1) + target_counts) * T + target
    for v in range(C):
        table[v] = jnp.max(jnp.where(held == v, codes, 0))

    token = lax.rem(lax.broadcasted_iota(jnp.int32, (1, rows), 1), I)

    def direct(t, carry):
        cq_copy(t).wait()
        total = jnp.zeros((1, hg * rows), jnp.float32)
        for g in range(G):
            queries = jnp.concatenate(
                [
                    cq_buf[t, :, (g * hg + q) * D : (g * hg + q + 1) * D]
                    for q in range(hg)
                ],
                axis=0,
            )
            scores = dot_nt(ts_buf[t, :, g * D : (g + 1) * D], queries)
            values = ud[g, pl.ds(pl.multiple_of(t * J, J), J), :]
            total = total + ratio(scores, values, lengths[t])
        tokens = total[:, 0:rows]
        for q in range(1, hg):
            tokens = tokens + total[:, q * rows : (q + 1) * rows]
        count = spread[pl.ds(t, 1), :]
        dsum[pl.ds(t, 1), :] = jnp.where(token < count, tokens, 0.0) / count.astype(jnp.float32)
        return carry

    lax.fori_loop(0, T, direct, 0)

    loads[3].wait()
    lanes = out.shape[1]
    direct_sums = dsum[...]
    owner = owners[...]
    rows_of = wide // rpp
    spot = lax.broadcasted_iota(jnp.int32, (T, wide), 1)
    for p in range(n):
        own = jnp.zeros((T, wide), jnp.float32)
        for r in range(rpp):
            part = jnp.where(owner == p * rpp + r, direct_sums, 0.0)
            part = jnp.sum(part, axis=1, keepdims=True)
            own = jnp.where(spot == r * rows_of, part, own)
        owns[p] = own
    RG = rpp * G
    key = lax.broadcasted_iota(jnp.int32, (I, hg * J), 0)
    row_of = lax.broadcasted_iota(jnp.int32, (RG, hg * J), 0) // G
    position = lax.rem(lax.broadcasted_iota(jnp.int32, (RG, hg * J), 1), J)
    row_of_sum = lax.broadcasted_iota(jnp.int32, (RG, wide), 0)
    own_lanes = lax.broadcasted_iota(jnp.int32, (RG, wide), 1) // hg == row_of_sum
    factor = math.log2(math.e) / math.sqrt(D)

    def lookup(p):
        return [table[p * rpp + r] for r in range(rpp)]

    def block(p, found):
        limits = jnp.zeros((RG, hg * J), jnp.int32)
        divisors = jnp.ones((RG, wide), jnp.float32)
        for r in range(rpp):
            t = lax.rem(found[r], T)
            target_count = lax.rem(found[r] // T, J + 1)
            source_count = found[r] // (T * (J + 1))
            limits = jnp.where(row_of == r, target_count, limits)
            divisors = jnp.where(
                row_of_sum // G == r, target_count.astype(jnp.float32), divisors
            )
            usable = key < source_count
            for g in range(G):
                queries = jnp.concatenate(
                    [
                        tq_buf[t, :, (g * hg + q) * D : (g * hg + q + 1) * D]
                        for q in range(hg)
                    ],
                    axis=0,
                )
                scores = dot_nt(k_buf[p, r, :, g * D : (g + 1) * D], queries)
                scores = jnp.where(usable, scores, masked_score)
                for c in range(0, hg * J, 128):
                    score[c // 128, pl.ds(r * G + g, I, stride=RG), :] = scores[:, c : c + 128]
        def at(k):
            return jnp.concatenate(
                [score[c, k * RG : (k + 1) * RG, :] for c in range(hg * J // 128)], axis=1
            )
        highest = at(0)
        for k in range(1, I):
            highest = jnp.maximum(highest, at(k))
        weights = [jnp.exp2((at(k) - highest) * factor) for k in range(I)]
        total = weights[0]
        for k in range(1, I):
            total = total + weights[k]
        scale = jnp.where(position < limits, 1.0 / total, 0.0)
        probs = jnp.concatenate(
            [(w * scale).astype(jnp.bfloat16) for w in weights], axis=0
        )
        sums = jnp.dot(probs, sel[...], preferred_element_type=jnp.float32)
        u = u_buf[p].astype(jnp.float32)
        mixed = sums[0:RG] * u[0:1]
        for k in range(1, I):
            mixed = mixed + sums[k * RG : (k + 1) * RG] * u[k : k + 1]
        mixed = jnp.where(own_lanes, mixed / divisors, 0.0)
        return jnp.sum(mixed, axis=0, keepdims=True) + jnp.sum(owns[p], axis=0, keepdims=True)

    u_buf[me] = u_out[me]
    loads[1].wait()
    r_buf[me] = block(me, lookup(me))

    def channel_step(i, carry):
        p = peers.arrival(i)
        found = lookup(p)
        k_copy(p, p).wait_recv()
        u_copy(p, p).wait_recv()
        r_out[p] = block(p, found)
        r_copy(p, me).start()

        return carry

    lax.fori_loop(0, n - 1, channel_step, 0)

    def settle(buffer, semaphore):
        rest = buffer.at[pl.ds(0, n - 1)]
        pltpu.make_async_copy(rest, rest, semaphore).wait()

    settle(r_buf, rr)
    settle(k_buf, ks)
    settle(u_buf, us)
    settle(r_buf, rs)
    sums = r_buf[...].reshape(n, wide)
    part = lax.broadcasted_iota(jnp.int32, (n, wide), 1) // rows_of
    place = lax.broadcasted_iota(jnp.int32, (n, lanes), 1)
    source = lax.broadcasted_iota(jnp.int32, (n, lanes), 0)
    result = jnp.zeros((n, lanes), jnp.float32)
    for r in range(rpp):
        value = jnp.sum(jnp.where(part == r, sums, 0.0), axis=1, keepdims=True)
        result = jnp.where(place == source * rpp + r, value, result)
    out[...] = jnp.sum(result, axis=0, keepdims=True)


def on_device(
    n,
    candidate_queries,
    target_states,
    target_queries,
    candidate_states,
    target_length,
    candidate_length,
    candidate_row,
    direct_readout,
    channel_readout,
):
    T, S, I, QW = candidate_queries.shape
    J = target_states.shape[1]
    H = QW // HEAD_SIZE
    G = target_states.shape[2] // (2 * HEAD_SIZE)
    C = T * S
    rpp = C // n
    hg = H // G
    wide = max(128, rpp * H)
    lanes = -(-C // 128) * 128
    bf, f32 = jnp.bfloat16, jnp.float32
    vmem, smem = pltpu.VMEM, pltpu.SMEM
    anywhere = pl.BlockSpec(memory_space=pl.ANY)
    dma = pltpu.SemaphoreType.DMA
    found = pl.pallas_call(
        functools.partial(kernel, n, (T, S, I, J, H, G)),
        out_shape=jax.ShapeDtypeStruct((1, lanes), f32),
        in_specs=[
            anywhere, anywhere, anywhere, anywhere, anywhere,
            anywhere, anywhere, anywhere, anywhere,
        ],
        out_specs=pl.BlockSpec(memory_space=vmem),
        scratch_shapes=[
            smem((T, S), jnp.int32),
            smem((T, S), jnp.int32),
            smem((T,), jnp.int32),
            smem((C,), jnp.int32),
            vmem((QW,), bf),
            vmem((QW,), bf),
            vmem((T, S * I, QW), bf),
            vmem(target_states.shape, bf),
            vmem(target_queries.shape, bf),
            vmem((n, rpp, I, G * HEAD_SIZE), bf),
            vmem((n, rpp, I, G * HEAD_SIZE), bf),
            vmem((n, I, wide), bf),
            vmem((n, I, wide), bf),
            vmem((T, S * I), jnp.int32),
            vmem((T, S * I), jnp.int32),
            vmem((G, T * J, hg * S * I), f32),
            vmem((hg * S * I, HEAD_SIZE), bf),
            vmem((hg * J, wide), bf),
            vmem((hg * J // 128, I * rpp * G, 128), f32),
            vmem((T, S), jnp.int32),
            vmem((T, S), jnp.int32),
            vmem((T, S * I), f32),
            vmem((n, T, wide), f32),
            vmem((n, 1, wide), f32),
            vmem((n, 1, wide), f32),
            dma((11,)), dma((T,)),
            dma, dma((n,)), dma, dma((n,)), dma, dma,
            pltpu.SemaphoreType.REGULAR,
        ],
        compiler_params=pltpu.CompilerParams(
            collective_id=0, has_side_effects=True, vmem_limit_bytes=60 << 20
        ),
    )(
        candidate_row, candidate_length, target_length,
        direct_readout, channel_readout,
        candidate_queries.reshape(T, S * I, QW),
        target_states, target_queries,
        candidate_states.reshape(n, rpp, I, 2 * G * HEAD_SIZE),
    )
    return found[0, :C]


def solution(mesh):
    in_specs = (
        P(("group", "dp"), None, None, None),
        P(("group", "dp"), None, None),
        P(("group", "dp"), None, None),
        P(("group", "dp"), None, None),
        P(("group", "dp")),
        P(("group", "dp"), None),
        P(("group", "dp"), None),
        P(),
        P(),
    )
    return jax.shard_map(
        functools.partial(on_device, mesh.shape[AXIS]),
        mesh=mesh, in_specs=in_specs, out_specs=P(("group", "dp")), check_vma=False,
    )
```

```python
import functools
import math

import jax
import jax.numpy as jnp
from jax import lax
from jax.experimental import pallas as pl
from jax.experimental.pallas import tpu as pltpu
from jax.sharding import PartitionSpec as P

HEAD_SIZE = 128
AXIS = "dp"
MESH = pl.DeviceIdType.MESH
EARLY = 2
HELD = 2
masked_score = -1e30


def dot_nt(a, b):
    return lax.dot_general(
        a, b, (((1,), (1,)), ((), ())), preferred_element_type=jnp.float32
    )


class Peers:
    def __init__(self, me, n):
        assert n >= 4 and n & (n - 1) == 0
        m = n // 4
        self.me, self.n, self.m = me, n, m
        self.quarter = lax.div(me, m)
        low = 1 - 2 * lax.rem(self.quarter, 2)
        high = 1 - 2 * lax.div(self.quarter, 2)
        self.outer = lax.rem(self.quarter + lax.div(self.quarter, 2), 2) == 0
        one, two = low * m, high * (2 * m)
        self.one, self.two, self.three = me + one, me + two, me + one + two
        self.far = lax.select(self.outer, self.three, self.two)
        self.near = lax.select(self.outer, self.two, self.three)
        steps, bit = [0], 1
        while bit < m:
            step = (1 - 2 * lax.rem(lax.div(me, bit), 2)) * bit
            steps = steps + [s + step for s in steps]
            bit *= 2
        self.steps = steps

    def inside(self):
        return [self.me + s for s in self.steps[1:]]

    def at(self, base):
        return [base + s for s in self.steps]

    def arrival(self, i):
        m = self.m
        i = i - (m - 1)
        early = lax.select(self.outer, 0, min(EARLY, m // 2))
        late = i - early
        part = lax.div(lax.max(late, 0), m)
        near = jnp.logical_or(late < 0, part == 2)
        one = part == lax.select(self.outer, 1, 0)
        j = lax.select(near, lax.select(late < 0, i, i - 2 * m), late - part * m)
        back = jnp.logical_not(jnp.logical_or(self.outer, jnp.logical_and(one, late >= 0)))
        j = lax.select(back, m - 1 - j, j)
        base = lax.select(one, self.one, self.far)
        base = lax.select(near, self.near, base)
        inside = i < 0
        base = lax.select(inside, self.me, base)
        j = lax.select(inside, i + m, j)
        peer, bit = base, 1
        while bit < m:
            step = (1 - 2 * lax.rem(lax.div(self.me, bit), 2)) * bit
            peer = peer + step * lax.rem(lax.div(j, bit), 2)
            bit *= 2
        return peer


def ratio(scores, values, keys_left):
    keys = lax.broadcasted_iota(jnp.int32, scores.shape, 0)
    scores = jnp.where(keys < keys_left, scores, masked_score)
    highest = jnp.max(scores, axis=0, keepdims=True)
    factor = math.log2(math.e) / math.sqrt(HEAD_SIZE)
    weights = jnp.exp2((scores - highest) * factor)
    return jnp.sum(weights * values, axis=0, keepdims=True) / jnp.sum(
        weights, axis=0, keepdims=True
    )


def kernel(
    n, dims,
    stored_in, sources_in, lengths_in, direct_in, channel_in, cq, ts, tq, cs,
    out,
    stored, sources, lengths, table, direct_r, channel_r,
    cq_buf, ts_buf, tq_buf, v_buf, k_buf, u_out, u_buf, spread, owners, ud, rd, sel, score, owned, owned_count, dsum, owns, r_out, r_buf,
    in_sem, cq_sem, ks, kr, us, ur, rs, rr, ready,
):
    T, S, I, J, H, G = dims
    C = T * S
    rpp = C // n
    hg = H // G
    D = HEAD_SIZE
    me = lax.axis_index(AXIS)

    loads = [
        pltpu.make_async_copy(cs.at[:, :, :, pl.ds(G * D, G * D)], v_buf, in_sem.at[0]),
        pltpu.make_async_copy(
            cs.at[me, :, :, pl.ds(0, G * D)], k_buf.at[me], in_sem.at[1]
        ),
        pltpu.make_async_copy(ts, ts_buf, in_sem.at[2]),
        pltpu.make_async_copy(tq, tq_buf, in_sem.at[3]),
        pltpu.make_async_copy(channel_in, channel_r, in_sem.at[4]),
        pltpu.make_async_copy(direct_in, direct_r, in_sem.at[5]),
        pltpu.make_async_copy(stored_in, stored, in_sem.at[6]),
        pltpu.make_async_copy(sources_in, sources, in_sem.at[7]),
        pltpu.make_async_copy(lengths_in, lengths, in_sem.at[8]),
        pltpu.make_async_copy(stored_in, owned, in_sem.at[9]),
        pltpu.make_async_copy(sources_in, owned_count, in_sem.at[10]),
    ]
    def cq_copy(t):
        return pltpu.make_async_copy(cq.at[t], cq_buf.at[t], cq_sem.at[t])

    barrier = pltpu.get_barrier_semaphore()
    peers = Peers(me, n)
    m = n // 4
    last = peers.quarter == 3

    def say(peer, semaphore):
        pl.semaphore_signal(
            semaphore, inc=1, device_id={AXIS: peer}, device_id_type=MESH
        )

    for peer in peers.inside():
        say(peer, barrier)
    cross = peers.at(peers.two) + peers.at(peers.three)

    @pl.when(jnp.logical_not(last))
    def _():
        for peer in cross + peers.at(peers.one):
            say(peer, barrier)

    for load in loads[4:]:
        load.start()
    loads[0].start()
    loads[2].start()
    cq_copy(0).start()

    def k_copy(p, slot):
        return pltpu.make_async_remote_copy(
            src_ref=cs.at[p, :, :, pl.ds(0, G * D)],
            dst_ref=k_buf.at[slot], send_sem=ks, recv_sem=kr.at[slot],
            device_id={AXIS: p}, device_id_type=MESH,
        )

    def u_copy(p, slot):
        return pltpu.make_async_remote_copy(
            src_ref=u_out.at[p], dst_ref=u_buf.at[slot], send_sem=us,
            recv_sem=ur.at[slot], device_id={AXIS: p}, device_id_type=MESH,
        )

    def r_copy(p, slot):
        return pltpu.make_async_remote_copy(
            src_ref=r_out.at[p], dst_ref=r_buf.at[slot], send_sem=rs,
            recv_sem=rr, device_id={AXIS: p}, device_id_type=MESH,
        )

    @pl.when(last)
    def _():
        pl.semaphore_wait(barrier, n - 1)
        for peer in cross + peers.at(peers.one):
            say(peer, ready)

    @pl.when(jnp.logical_not(last))
    def _():
        pl.semaphore_wait(barrier, n - 1 - m)

    early = min(EARLY, m // 2)
    far = peers.at(peers.far)
    near = peers.at(peers.near)[::-1]
    for peer in near[:early]:
        k_copy(peer, me).start()
    loads[1].start()
    for t in range(1, T):
        cq_copy(t).start()
    loads[3].start()

    wide = u_out.shape[2]
    head_id = lax.broadcasted_iota(jnp.int32, (H, D), 0)
    rows_r = jnp.zeros((H, D), jnp.float32)
    loads[4].wait()
    for h in range(H):
        row = channel_r[h * D : (h + 1) * D].astype(jnp.float32).reshape(1, D)
        rows_r = jnp.where(head_id == h, row, rows_r)
    rows_r = jnp.concatenate([rows_r.astype(jnp.bfloat16)] * (wide // H), axis=0)
    row_id = lax.broadcasted_iota(jnp.int32, (wide, D), 0)
    loads[0].wait()
    u = None
    for r in range(rpp):
        for g in range(G):
            weights = jnp.where(
                row_id // hg == r * G + g, rows_r, jnp.zeros_like(rows_r)
            )
            values = v_buf[:, r, :, g * D : (g + 1) * D]
            values = values.reshape(n * I, D)
            part = dot_nt(values, weights)
            u = part if u is None else u + part
    turn = lax.rem(lax.broadcasted_iota(jnp.int32, u.shape, 1), hg)
    for q in range(1, hg):
        error = u - u.astype(jnp.bfloat16).astype(jnp.float32)
        u = jnp.where(turn == q, u + pltpu.roll(error, 1, 1), u)
    u_out[...] = u.astype(jnp.bfloat16).reshape(n, I, wide)

    lane = lax.broadcasted_iota(jnp.int32, (hg * J, wide), 1)
    head = lax.broadcasted_iota(jnp.int32, (hg * J, wide), 0) // J
    sel[...] = jnp.where(lax.rem(lane, hg) == head, 1.0, 0.0).astype(jnp.bfloat16)

    @pl.when(jnp.logical_not(last))
    def _():
        pl.semaphore_wait(ready, m)

    other = peers.inside() + peers.at(peers.one)
    for peer in near[:early] + far + near[early:] + other:
        u_copy(peer, me).start()
    back = near[max(early, m - HELD) :]
    for peer in far + near[early : max(early, m - HELD)] + other:
        k_copy(peer, me).start()

    for peer in back:
        k_copy(peer, me).start()

    rows = S * I
    slot = lax.broadcasted_iota(jnp.int32, (1, rows), 1) // I
    for load in loads[5:]:
        load.wait()
    for t in range(T):
        held = jnp.zeros((1, rows), jnp.int32)
        count = jnp.zeros((1, rows), jnp.int32)
        for c in range(S):
            held = jnp.where(slot == c, stored[t, c], held)
            count = jnp.where(slot == c, sources[t, c], count)
        owners[t : t + 1, :] = held
        spread[t : t + 1, :] = count

    loads[2].wait()
    for g in range(G):
        states = ts_buf[:, :, (G + g) * D : (G + g + 1) * D].reshape(T * J, D)
        for q in range(hg):
            h = g * hg + q
            rd[q * rows : (q + 1) * rows, :] = jnp.broadcast_to(
                direct_r[h * D : (h + 1) * D].astype(jnp.float32).reshape(1, D), (rows, D)
            ).astype(jnp.bfloat16)
        ud[g] = dot_nt(states, rd[...])

    held = owned[...]
    target = lax.broadcasted_iota(jnp.int32, (T, S), 0)
    target_counts = jnp.zeros((T, S), jnp.int32)
    for t in range(T):
        target_counts = jnp.where(target == t, lengths[t], target_counts)
    base, step = 1 << J.bit_length(), 1 << (T - 1).bit_length()
    codes = (owned_count[...] * base + target_counts) * step + target
    for v in range(C):
        table[v] = jnp.max(jnp.where(held == v, codes, 0))

    token = lax.rem(lax.broadcasted_iota(jnp.int32, (1, rows), 1), I)

    def direct(t, carry):
        cq_copy(t).wait()
        total = jnp.zeros((1, hg * rows), jnp.float32)
        for g in range(G):
            queries = jnp.concatenate(
                [
                    cq_buf[t, :, (g * hg + q) * D : (g * hg + q + 1) * D]
                    for q in range(hg)
                ],
                axis=0,
            )
            scores = dot_nt(ts_buf[t, :, g * D : (g + 1) * D], queries)
            values = ud[g, pl.ds(pl.multiple_of(t * J, J), J), :]
            total = total + ratio(scores, values, lengths[t])
        tokens = total[:, 0:rows]
        for q in range(1, hg):
            tokens = tokens + total[:, q * rows : (q + 1) * rows]
        count = spread[pl.ds(t, 1), :]
        dsum[pl.ds(t, 1), :] = jnp.where(token < count, tokens, 0.0) / count.astype(jnp.float32)
        return carry

    lax.fori_loop(0, T, direct, 0)

    loads[3].wait()
    lanes = out.shape[1]
    direct_sums = dsum[...]
    owner = owners[...]
    rows_of = wide // rpp
    spot = lax.broadcasted_iota(jnp.int32, (T, wide), 1)
    for p in range(n):
        own = jnp.zeros((T, wide), jnp.float32)
        for r in range(rpp):
            part = jnp.where(owner == p * rpp + r, direct_sums, 0.0)
            part = jnp.sum(part, axis=1, keepdims=True)
            own = jnp.where(spot == r * rows_of, part, own)
        owns[p] = own
    RG = rpp * G
    key = lax.broadcasted_iota(jnp.int32, (I, hg * J), 0)
    row_of = lax.broadcasted_iota(jnp.int32, (RG, hg * J), 0) // G
    position = lax.rem(lax.broadcasted_iota(jnp.int32, (RG, hg * J), 1), J)
    row_of_sum = lax.broadcasted_iota(jnp.int32, (RG, wide), 0)
    own_lanes = lax.broadcasted_iota(jnp.int32, (RG, wide), 1) // hg == row_of_sum
    factor = math.log2(math.e) / math.sqrt(D)

    def lookup(p):
        targets, counts = [], []
        limits = jnp.zeros((RG, hg * J), jnp.int32)
        for r in range(rpp):
            code = table[p * rpp + r]
            targets.append(lax.rem(code, step))
            counts.append(lax.div(code, base * step))
            limits = jnp.where(row_of == r, lax.rem(lax.div(code, step), base), limits)
        kept = position < limits
        shares = jnp.where(own_lanes, 1.0 / limits[:, :wide].astype(jnp.float32), 0.0)
        own = jnp.sum(owns[p], axis=0, keepdims=True)
        return targets, counts, kept, shares, own

    def block(p, found):
        targets, counts, kept, shares, own = found
        for r in range(rpp):
            t = targets[r]
            source_count = counts[r]
            usable = key < source_count
            for g in range(G):
                queries = jnp.concatenate(
                    [
                        tq_buf[t, :, (g * hg + q) * D : (g * hg + q + 1) * D]
                        for q in range(hg)
                    ],
                    axis=0,
                )
                scores = dot_nt(k_buf[p, r, :, g * D : (g + 1) * D], queries)
                scores = jnp.where(usable, scores, masked_score)
                for c in range(0, hg * J, 128):
                    score[c // 128, pl.ds(r * G + g, I, stride=RG), :] = scores[:, c : c + 128]
        def at(k):
            return jnp.concatenate(
                [score[c, k * RG : (k + 1) * RG, :] for c in range(hg * J // 128)], axis=1
            )
        highest = at(0)
        for k in range(1, I):
            highest = jnp.maximum(highest, at(k))
        weights = [jnp.exp2((at(k) - highest) * factor) for k in range(I)]
        total = weights[0]
        for k in range(1, I):
            total = total + weights[k]
        scale = jnp.where(kept, 1.0 / total, 0.0)
        probs = jnp.concatenate(
            [(w * scale).astype(jnp.bfloat16) for w in weights], axis=0
        )
        sums = jnp.dot(probs, sel[...], preferred_element_type=jnp.float32)
        u = u_buf[p].astype(jnp.float32)
        mixed = sums[0:RG] * u[0:1]
        for k in range(1, I):
            mixed = mixed + sums[k * RG : (k + 1) * RG] * u[k : k + 1]
        return jnp.sum(mixed * shares, axis=0, keepdims=True) + own

    u_buf[me] = u_out[me]
    loads[1].wait()
    r_buf[me] = block(me, lookup(me))

    def channel_step(i, carry):
        p = peers.arrival(i)
        found = lookup(p)
        k_copy(p, p).wait_recv()
        u_copy(p, p).wait_recv()
        r_out[p] = block(p, found)
        r_copy(p, me).start()

        return carry

    lax.fori_loop(0, n - 1, channel_step, 0)

    def settle(buffer, semaphore):
        rest = buffer.at[pl.ds(0, n - 1)]
        pltpu.make_async_copy(rest, rest, semaphore).wait()

    settle(r_buf, rr)
    settle(k_buf, ks)
    settle(u_buf, us)
    settle(r_buf, rs)
    sums = r_buf[...].reshape(n, wide)
    part = lax.broadcasted_iota(jnp.int32, (n, wide), 1) // rows_of
    place = lax.broadcasted_iota(jnp.int32, (n, lanes), 1)
    source = lax.broadcasted_iota(jnp.int32, (n, lanes), 0)
    result = jnp.zeros((n, lanes), jnp.float32)
    for r in range(rpp):
        value = jnp.sum(jnp.where(part == r, sums, 0.0), axis=1, keepdims=True)
        result = jnp.where(place == source * rpp + r, value, result)
    out[...] = jnp.sum(result, axis=0, keepdims=True)


def on_device(
    n,
    candidate_queries,
    target_states,
    target_queries,
    candidate_states,
    target_length,
    candidate_length,
    candidate_row,
    direct_readout,
    channel_readout,
):
    T, S, I, QW = candidate_queries.shape
    J = target_states.shape[1]
    H = QW // HEAD_SIZE
    G = target_states.shape[2] // (2 * HEAD_SIZE)
    C = T * S
    rpp = C // n
    hg = H // G
    wide = max(128, rpp * H)
    lanes = -(-C // 128) * 128
    bf, f32 = jnp.bfloat16, jnp.float32
    vmem, smem = pltpu.VMEM, pltpu.SMEM
    anywhere = pl.BlockSpec(memory_space=pl.ANY)
    dma = pltpu.SemaphoreType.DMA
    found = pl.pallas_call(
        functools.partial(kernel, n, (T, S, I, J, H, G)),
        out_shape=jax.ShapeDtypeStruct((1, lanes), f32),
        in_specs=[
            anywhere, anywhere, anywhere, anywhere, anywhere,
            anywhere, anywhere, anywhere, anywhere,
        ],
        out_specs=pl.BlockSpec(memory_space=vmem),
        scratch_shapes=[
            smem((T, S), jnp.int32),
            smem((T, S), jnp.int32),
            smem((T,), jnp.int32),
            smem((C,), jnp.int32),
            vmem((QW,), bf),
            vmem((QW,), bf),
            vmem((T, S * I, QW), bf),
            vmem(target_states.shape, bf),
            vmem(target_queries.shape, bf),
            vmem((n, rpp, I, G * HEAD_SIZE), bf),
            vmem((n, rpp, I, G * HEAD_SIZE), bf),
            vmem((n, I, wide), bf),
            vmem((n, I, wide), bf),
            vmem((T, S * I), jnp.int32),
            vmem((T, S * I), jnp.int32),
            vmem((G, T * J, hg * S * I), f32),
            vmem((hg * S * I, HEAD_SIZE), bf),
            vmem((hg * J, wide), bf),
            vmem((hg * J // 128, I * rpp * G, 128), f32),
            vmem((T, S), jnp.int32),
            vmem((T, S), jnp.int32),
            vmem((T, S * I), f32),
            vmem((n, T, wide), f32),
            vmem((n, 1, wide), f32),
            vmem((n, 1, wide), f32),
            dma((11,)), dma((T,)),
            dma, dma((n,)), dma, dma((n,)), dma, dma,
            pltpu.SemaphoreType.REGULAR,
        ],
        compiler_params=pltpu.CompilerParams(
            collective_id=0, has_side_effects=True, vmem_limit_bytes=56553472
        ),
    )(
        candidate_row, candidate_length, target_length,
        direct_readout, channel_readout,
        candidate_queries.reshape(T, S * I, QW),
        target_states, target_queries,
        candidate_states.reshape(n, rpp, I, 2 * G * HEAD_SIZE),
    )
    return found[0, :C]


def solution(mesh):
    in_specs = (
        P(("group", "dp"), None, None, None),
        P(("group", "dp"), None, None),
        P(("group", "dp"), None, None),
        P(("group", "dp"), None, None),
        P(("group", "dp")),
        P(("group", "dp"), None),
        P(("group", "dp"), None),
        P(),
        P(),
    )
    return jax.shard_map(
        functools.partial(on_device, mesh.shape[AXIS]),
        mesh=mesh, in_specs=in_specs, out_specs=P(("group", "dp")), check_vma=False,
    )
```

```python
import functools
import math

import jax
import jax.numpy as jnp
from jax import lax
from jax.experimental import pallas as pl
from jax.experimental.pallas import tpu as pltpu
from jax.sharding import PartitionSpec as P

HEAD_SIZE = 128
AXIS = "dp"
MESH = pl.DeviceIdType.MESH
masked_score = -1e30


def dot_nt(a, b):
    return lax.dot_general(
        a, b, (((1,), (1,)), ((), ())), preferred_element_type=jnp.float32
    )


class Peers:
    def __init__(self, me, n):
        assert n >= 8 and n & (n - 1) == 0
        m = n // 4
        self.me, self.n, self.m = me, n, m
        self.quarter = lax.div(me, m)
        low = 1 - 2 * lax.rem(self.quarter, 2)
        high = 1 - 2 * lax.div(self.quarter, 2)
        self.outer = lax.rem(self.quarter + lax.div(self.quarter, 2), 2) == 0
        one, two = low * m, high * (2 * m)
        self.one, self.two, self.three = me + one, me + two, me + one + two
        self.far = lax.select(self.outer, self.three, self.two)
        self.near = lax.select(self.outer, self.two, self.three)
        steps, bit = [0], 1
        while bit < m:
            step = (1 - 2 * lax.rem(lax.div(me, bit), 2)) * bit
            steps = steps + [s + step for s in steps]
            bit *= 2
        self.steps = steps

    def place(self, k):
        m = self.m
        return m // 2 - 1 if k == 0 else m - k - (m // 2 - 1 + k) // m

    def inside(self):
        return [self.me + s for s in self.steps[1:]]

    def at(self, base):
        return [base + s for s in self.steps]

    def arrival(self, i):
        m = self.m
        i = i - (m - 1)
        early = lax.select(self.outer, 0, 1)
        late = i - early
        part = lax.div(lax.max(late, 0), m)
        near = jnp.logical_or(late < 0, part == 2)
        one = part == lax.select(self.outer, 1, 0)
        j = lax.select(near, lax.select(late < 0, i, i - 2 * m), late - part * m)
        one = jnp.logical_and(one, late >= 0)
        back = lax.select(near, lax.select(j == 0, m // 2 - 1, m - j - lax.div(m // 2 - 1 + j, m)), m - 1 - j)
        j = lax.select(jnp.logical_or(self.outer, one), j, back)
        base = lax.select(one, self.one, self.far)
        base = lax.select(near, self.near, base)
        inside = i < 0
        base = lax.select(inside, self.me, base)
        j = lax.select(inside, i + m, j)
        peer, bit = base, 1
        while bit < m:
            step = (1 - 2 * lax.rem(lax.div(self.me, bit), 2)) * bit
            peer = peer + step * lax.rem(lax.div(j, bit), 2)
            bit *= 2
        return peer


def ratio(scores, values, keys_left):
    keys = lax.broadcasted_iota(jnp.int32, scores.shape, 0)
    scores = jnp.where(keys < keys_left, scores, masked_score)
    highest = jnp.max(scores, axis=0, keepdims=True)
    factor = math.log2(math.e) / math.sqrt(HEAD_SIZE)
    weights = jnp.exp2((scores - highest) * factor)
    return jnp.sum(weights * values, axis=0, keepdims=True) / jnp.sum(
        weights, axis=0, keepdims=True
    )


def kernel(
    n, dims,
    stored_in, sources_in, lengths_in, direct_in, channel_in, cq, ts, tq, cs,
    out,
    stored, sources, lengths, table, direct_r, channel_r,
    cq_buf, ts_buf, tq_buf, v_buf, k_buf, u_out, u_buf, spread, owners, ud, rd, sel, score, owned, owned_count, dsum, owns, r_out, r_buf,
    in_sem, cq_sem, ks, kr, us, ur, rs, rr, ready,
):
    T, S, I, J, H, G = dims
    C = T * S
    rpp = C // n
    hg = H // G
    D = HEAD_SIZE
    me = lax.axis_index(AXIS)

    loads = [
        pltpu.make_async_copy(cs.at[:, :, :, pl.ds(G * D, G * D)], v_buf, in_sem.at[0]),
        pltpu.make_async_copy(
            cs.at[me, :, :, pl.ds(0, G * D)], k_buf.at[me], in_sem.at[1]
        ),
        pltpu.make_async_copy(ts, ts_buf, in_sem.at[2]),
        pltpu.make_async_copy(tq, tq_buf, in_sem.at[3]),
        pltpu.make_async_copy(channel_in, channel_r, in_sem.at[4]),
        pltpu.make_async_copy(direct_in, direct_r, in_sem.at[5]),
        pltpu.make_async_copy(stored_in, stored, in_sem.at[6]),
        pltpu.make_async_copy(sources_in, sources, in_sem.at[7]),
        pltpu.make_async_copy(lengths_in, lengths, in_sem.at[8]),
        pltpu.make_async_copy(stored_in, owned, in_sem.at[9]),
        pltpu.make_async_copy(sources_in, owned_count, in_sem.at[10]),
    ]
    def cq_copy(t):
        return pltpu.make_async_copy(cq.at[t], cq_buf.at[t], cq_sem.at[t])

    barrier = pltpu.get_barrier_semaphore()
    peers = Peers(me, n)
    m = n // 4
    last = peers.quarter == 3

    def say(peer, semaphore):
        pl.semaphore_signal(
            semaphore, inc=1, device_id={AXIS: peer}, device_id_type=MESH
        )

    opens = peers.quarter == 0
    middle = jnp.logical_not(jnp.logical_or(opens, last))
    cross = peers.at(peers.two) + peers.at(peers.three)

    half = m // 2
    ahead = lax.rem(lax.div(me, half), 2) == 0
    first = jnp.logical_and(middle, ahead)
    second = jnp.logical_and(middle, jnp.logical_not(ahead))
    across = [base + step for base in (peers.three, me) for step in peers.steps[half:]]

    @pl.when(middle)
    def _():
        for peer in peers.at(peers.three)[:half] + peers.at(peers.one) + peers.at(peers.two):
            say(peer, barrier)
        for peer in peers.inside()[: half - 1]:
            say(peer, barrier)

    @pl.when(first)
    def _():
        for peer in across:
            say(peer, barrier)

    @pl.when(opens)
    def _():
        for peer in peers.at(peers.three):
            say(peer, barrier)

    @pl.when(jnp.logical_not(middle))
    def _():
        for peer in peers.inside():
            say(peer, barrier)

    for load in loads[4:]:
        load.start()
    loads[0].start()
    loads[2].start()
    cq_copy(0).start()

    def k_copy(p, slot):
        return pltpu.make_async_remote_copy(
            src_ref=cs.at[p, :, :, pl.ds(0, G * D)],
            dst_ref=k_buf.at[slot], send_sem=ks, recv_sem=kr.at[slot],
            device_id={AXIS: p}, device_id_type=MESH,
        )

    def u_copy(p, slot):
        return pltpu.make_async_remote_copy(
            src_ref=u_out.at[p], dst_ref=u_buf.at[slot], send_sem=us,
            recv_sem=ur.at[slot], device_id={AXIS: p}, device_id_type=MESH,
        )

    def r_copy(p, slot):
        return pltpu.make_async_remote_copy(
            src_ref=r_out.at[p], dst_ref=r_buf.at[slot], send_sem=rs,
            recv_sem=rr, device_id={AXIS: p}, device_id_type=MESH,
        )

    @pl.when(last)
    def _():
        pl.semaphore_wait(barrier, n - 1)
        for peer in cross + peers.at(peers.one):
            say(peer, ready)

    @pl.when(opens)
    def _():
        pl.semaphore_wait(barrier, n - 1 - m)
        for peer in peers.at(peers.one) + peers.at(peers.two):
            say(peer, ready)

    @pl.when(first)
    def _():
        pl.semaphore_wait(barrier, m - 1)

    @pl.when(second)
    def _():
        pl.semaphore_wait(barrier, 2 * m - 1)
        for peer in across:
            say(peer, ready)

    far = peers.at(peers.far)
    near = [
        peers.near + lax.select(peers.outer, peers.steps[m - 1 - k], peers.steps[peers.place(k)])
        for k in range(m)
    ]
    k_copy(near[0], me).start()

    @pl.when(peers.outer)
    def _():
        k_copy(near[1], me).start()

    loads[1].start()
    for t in range(1, T):
        cq_copy(t).start()
    loads[3].start()

    wide = u_out.shape[2]
    head_id = lax.broadcasted_iota(jnp.int32, (H, D), 0)
    rows_r = jnp.zeros((H, D), jnp.float32)
    loads[4].wait()
    for h in range(H):
        row = channel_r[h * D : (h + 1) * D].astype(jnp.float32).reshape(1, D)
        rows_r = jnp.where(head_id == h, row, rows_r)
    rows_r = jnp.concatenate([rows_r.astype(jnp.bfloat16)] * (wide // H), axis=0)
    row_id = lax.broadcasted_iota(jnp.int32, (wide, D), 0)
    loads[0].wait()
    u = None
    for r in range(rpp):
        for g in range(G):
            weights = jnp.where(
                row_id // hg == r * G + g, rows_r, jnp.zeros_like(rows_r)
            )
            values = v_buf[:, r, :, g * D : (g + 1) * D]
            values = values.reshape(n * I, D)
            part = dot_nt(values, weights)
            u = part if u is None else u + part
    turn = lax.rem(lax.broadcasted_iota(jnp.int32, u.shape, 1), hg)
    for q in range(1, hg):
        error = u - u.astype(jnp.bfloat16).astype(jnp.float32)
        u = jnp.where(turn == q, u + pltpu.roll(error, 1, 1), u)
    u_out[...] = u.astype(jnp.bfloat16).reshape(n, I, wide)

    lane = lax.broadcasted_iota(jnp.int32, (hg * J, wide), 1)
    head = lax.broadcasted_iota(jnp.int32, (hg * J, wide), 0) // J
    sel[...] = jnp.where(lax.rem(lane, hg) == head, 1.0, 0.0).astype(jnp.bfloat16)

    @pl.when(opens)
    def _():
        pl.semaphore_wait(ready, m)

    @pl.when(first)
    def _():
        pl.semaphore_wait(ready, 3 * m)

    @pl.when(second)
    def _():
        pl.semaphore_wait(ready, 2 * m)

    other = peers.inside() + peers.at(peers.one)
    for peer in near[:2] + far + near[2:] + other:
        u_copy(peer, me).start()
    for peer in far:
        k_copy(peer, me).start()

    @pl.when(jnp.logical_not(peers.outer))
    def _():
        k_copy(near[1], me).start()

    for peer in near[2:] + other:
        k_copy(peer, me).start()

    rows = S * I
    slot = lax.broadcasted_iota(jnp.int32, (1, rows), 1) // I
    for load in loads[5:]:
        load.wait()
    for t in range(T):
        held = jnp.zeros((1, rows), jnp.int32)
        count = jnp.zeros((1, rows), jnp.int32)
        for c in range(S):
            held = jnp.where(slot == c, stored[t, c], held)
            count = jnp.where(slot == c, sources[t, c], count)
        owners[t : t + 1, :] = held
        spread[t : t + 1, :] = count

    loads[2].wait()
    for g in range(G):
        states = ts_buf[:, :, (G + g) * D : (G + g + 1) * D].reshape(T * J, D)
        for q in range(hg):
            h = g * hg + q
            rd[q * rows : (q + 1) * rows, :] = jnp.broadcast_to(
                direct_r[h * D : (h + 1) * D].astype(jnp.float32).reshape(1, D), (rows, D)
            ).astype(jnp.bfloat16)
        ud[g] = dot_nt(states, rd[...])

    held = owned[...]
    target = lax.broadcasted_iota(jnp.int32, (T, S), 0)
    target_counts = jnp.zeros((T, S), jnp.int32)
    for t in range(T):
        target_counts = jnp.where(target == t, lengths[t], target_counts)
    base, step = 1 << J.bit_length(), 1 << (T - 1).bit_length()
    codes = (owned_count[...] * base + target_counts) * step + target
    for v in range(C):
        table[v] = jnp.max(jnp.where(held == v, codes, 0))

    token = lax.rem(lax.broadcasted_iota(jnp.int32, (1, rows), 1), I)

    def direct(t, carry):
        cq_copy(t).wait()
        total = jnp.zeros((1, hg * rows), jnp.float32)
        for g in range(G):
            queries = jnp.concatenate(
                [
                    cq_buf[t, :, (g * hg + q) * D : (g * hg + q + 1) * D]
                    for q in range(hg)
                ],
                axis=0,
            )
            scores = dot_nt(ts_buf[t, :, g * D : (g + 1) * D], queries)
            values = ud[g, pl.ds(pl.multiple_of(t * J, J), J), :]
            total = total + ratio(scores, values, lengths[t])
        tokens = total[:, 0:rows]
        for q in range(1, hg):
            tokens = tokens + total[:, q * rows : (q + 1) * rows]
        count = spread[pl.ds(t, 1), :]
        dsum[pl.ds(t, 1), :] = jnp.where(token < count, tokens, 0.0) / count.astype(jnp.float32)
        return carry

    lax.fori_loop(0, T, direct, 0)

    loads[3].wait()
    lanes = out.shape[0]
    direct_sums = dsum[...]
    owner = owners[...]
    rows_of = wide // rpp
    spot = lax.broadcasted_iota(jnp.int32, (T, wide), 1)
    for p in range(n):
        own = jnp.zeros((T, wide), jnp.float32)
        for r in range(rpp):
            part = jnp.where(owner == p * rpp + r, direct_sums, 0.0)
            part = jnp.sum(part, axis=1, keepdims=True)
            own = jnp.where(spot == r * rows_of, part, own)
        owns[p] = own
    RG = rpp * G
    key = lax.broadcasted_iota(jnp.int32, (I, hg * J), 0)
    row_of = lax.broadcasted_iota(jnp.int32, (RG, hg * J), 0) // G
    position = lax.rem(lax.broadcasted_iota(jnp.int32, (RG, hg * J), 1), J)
    row_of_sum = lax.broadcasted_iota(jnp.int32, (RG, wide), 0)
    own_lanes = lax.broadcasted_iota(jnp.int32, (RG, wide), 1) // hg == row_of_sum
    factor = math.log2(math.e) / math.sqrt(D)

    def lookup(p):
        targets, counts = [], []
        limits = jnp.zeros((RG, hg * J), jnp.int32)
        for r in range(rpp):
            code = table[p * rpp + r]
            targets.append(lax.rem(code, step))
            counts.append(lax.div(code, base * step))
            limits = jnp.where(row_of == r, lax.rem(lax.div(code, step), base), limits)
        kept = position < limits
        shares = jnp.where(own_lanes, 1.0 / limits[:, :wide].astype(jnp.float32), 0.0)
        own = jnp.sum(owns[p], axis=0, keepdims=True)
        return targets, counts, kept, shares, own

    def block(p, found):
        targets, counts, kept, shares, own = found
        for r in range(rpp):
            t = targets[r]
            source_count = counts[r]
            usable = key < source_count
            for g in range(G):
                queries = jnp.concatenate(
                    [
                        tq_buf[t, :, (g * hg + q) * D : (g * hg + q + 1) * D]
                        for q in range(hg)
                    ],
                    axis=0,
                )
                scores = dot_nt(k_buf[p, r, :, g * D : (g + 1) * D], queries)
                scores = jnp.where(usable, scores, masked_score)
                for c in range(0, hg * J, 128):
                    score[c // 128, pl.ds(r * G + g, I, stride=RG), :] = scores[:, c : c + 128]
        def at(k):
            return jnp.concatenate(
                [score[c, k * RG : (k + 1) * RG, :] for c in range(hg * J // 128)], axis=1
            )
        highest = at(0)
        for k in range(1, I):
            highest = jnp.maximum(highest, at(k))
        weights = [jnp.exp2((at(k) - highest) * factor) for k in range(I)]
        total = weights[0]
        for k in range(1, I):
            total = total + weights[k]
        scale = jnp.where(kept, 1.0 / total, 0.0)
        probs = jnp.concatenate(
            [(w * scale).astype(jnp.bfloat16) for w in weights], axis=0
        )
        sums = jnp.dot(probs, sel[...], preferred_element_type=jnp.float32)
        u = u_buf[p].astype(jnp.float32)
        mixed = sums[0:RG] * u[0:1]
        for k in range(1, I):
            mixed = mixed + sums[k * RG : (k + 1) * RG] * u[k : k + 1]
        return jnp.sum(mixed * shares, axis=0, keepdims=True) + own

    u_buf[me] = u_out[me]
    loads[1].wait()
    r_buf[me] = block(me, lookup(me))

    def channel_step(i, carry):
        p = peers.arrival(i)
        found = lookup(p)
        k_copy(p, p).wait_recv()
        u_copy(p, p).wait_recv()
        r_out[p] = block(p, found)
        r_copy(p, me).start()

        return carry

    lax.fori_loop(0, n - 1, channel_step, 0)

    def settle(buffer, semaphore):
        rest = buffer.at[pl.ds(0, n - 1)]
        pltpu.make_async_copy(rest, rest, semaphore).wait()

    settle(r_buf, rr)
    settle(k_buf, ks)
    settle(u_buf, us)
    settle(r_buf, rs)
    sums = r_buf[...].reshape(n, wide)
    part = lax.broadcasted_iota(jnp.int32, (n, wide), 1) // rows_of
    place = lax.broadcasted_iota(jnp.int32, (n, lanes), 1)
    source = lax.broadcasted_iota(jnp.int32, (n, lanes), 0)
    result = jnp.zeros((n, lanes), jnp.float32)
    for r in range(rpp):
        value = jnp.sum(jnp.where(part == r, sums, 0.0), axis=1, keepdims=True)
        result = jnp.where(place == source * rpp + r, value, result)
    out[...] = jnp.sum(result, axis=0)


def on_device(
    n,
    candidate_queries,
    target_states,
    target_queries,
    candidate_states,
    target_length,
    candidate_length,
    candidate_row,
    direct_readout,
    channel_readout,
):
    T, S, I, QW = candidate_queries.shape
    J = target_states.shape[1]
    H = QW // HEAD_SIZE
    G = target_states.shape[2] // (2 * HEAD_SIZE)
    C = T * S
    rpp = C // n
    hg = H // G
    wide = max(128, rpp * H)
    lanes = -(-C // 128) * 128
    bf, f32 = jnp.bfloat16, jnp.float32
    vmem, smem = pltpu.VMEM, pltpu.SMEM
    anywhere = pl.BlockSpec(memory_space=pl.ANY)
    dma = pltpu.SemaphoreType.DMA
    found = pl.pallas_call(
        functools.partial(kernel, n, (T, S, I, J, H, G)),
        out_shape=jax.ShapeDtypeStruct((C,), f32),
        in_specs=[
            anywhere, anywhere, anywhere, anywhere, anywhere,
            anywhere, anywhere, anywhere, anywhere,
        ],
        out_specs=pl.BlockSpec(memory_space=vmem),
        scratch_shapes=[
            smem((T, S), jnp.int32),
            smem((T, S), jnp.int32),
            smem((T,), jnp.int32),
            smem((C,), jnp.int32),
            vmem((QW,), bf),
            vmem((QW,), bf),
            vmem((T, S * I, QW), bf),
            vmem(target_states.shape, bf),
            vmem(target_queries.shape, bf),
            vmem((n, rpp, I, G * HEAD_SIZE), bf),
            vmem((n, rpp, I, G * HEAD_SIZE), bf),
            vmem((n, I, wide), bf),
            vmem((n, I, wide), bf),
            vmem((T, S * I), jnp.int32),
            vmem((T, S * I), jnp.int32),
            vmem((G, T * J, hg * S * I), f32),
            vmem((hg * S * I, HEAD_SIZE), bf),
            vmem((hg * J, wide), bf),
            vmem((hg * J // 128, I * rpp * G, 128), f32),
            vmem((T, S), jnp.int32),
            vmem((T, S), jnp.int32),
            vmem((T, S * I), f32),
            vmem((n, T, wide), f32),
            vmem((n, 1, wide), f32),
            vmem((n, 1, wide), f32),
            dma((11,)), dma((T,)),
            dma, dma((n,)), dma, dma((n,)), dma, dma,
            pltpu.SemaphoreType.REGULAR,
        ],
        compiler_params=pltpu.CompilerParams(
            collective_id=0, has_side_effects=True, vmem_limit_bytes=56553472
        ),
    )(
        candidate_row, candidate_length, target_length,
        direct_readout, channel_readout,
        candidate_queries.reshape(T, S * I, QW),
        target_states, target_queries,
        candidate_states.reshape(n, rpp, I, 2 * G * HEAD_SIZE),
    )
    return found


def solution(mesh):
    in_specs = (
        P(("group", "dp"), None, None, None),
        P(("group", "dp"), None, None),
        P(("group", "dp"), None, None),
        P(("group", "dp"), None, None),
        P(("group", "dp")),
        P(("group", "dp"), None),
        P(("group", "dp"), None),
        P(),
        P(),
    )
    return jax.shard_map(
        functools.partial(on_device, mesh.shape[AXIS]),
        mesh=mesh, in_specs=in_specs, out_specs=P(("group", "dp")), check_vma=False,
    )
```

```python
import functools
import math

import jax
import jax.numpy as jnp
from jax import lax
from jax.experimental import pallas as pl
from jax.experimental.pallas import tpu as pltpu
from jax.sharding import PartitionSpec as P

HEAD_SIZE = 128
AXIS = "dp"
MESH = pl.DeviceIdType.MESH
masked_score = -1e30


def dot_nt(a, b):
    return lax.dot_general(
        a, b, (((1,), (1,)), ((), ())), preferred_element_type=jnp.float32
    )


class Peers:
    def __init__(self, me, n):
        assert n >= 8 and n & (n - 1) == 0
        m = n // 4
        self.me, self.n, self.m = me, n, m
        self.quarter = lax.div(me, m)
        low = 1 - 2 * lax.rem(self.quarter, 2)
        high = 1 - 2 * lax.div(self.quarter, 2)
        self.outer = lax.rem(self.quarter + lax.div(self.quarter, 2), 2) == 0
        one, two = low * m, high * (2 * m)
        self.one, self.two, self.three = me + one, me + two, me + one + two
        self.far = lax.select(self.outer, self.three, self.two)
        self.near = lax.select(self.outer, self.two, self.three)
        steps, bit = [0], 1
        while bit < m:
            step = (1 - 2 * lax.rem(lax.div(me, bit), 2)) * bit
            steps = steps + [s + step for s in steps]
            bit *= 2
        self.steps = steps

    def place(self, k):
        m = self.m
        return m // 2 - 1 if k == 0 else m - k - (m // 2 - 1 + k) // m

    def inside(self):
        return [self.me + s for s in self.steps[1:]]

    def at(self, base):
        return [base + s for s in self.steps]

    def arrival(self, i):
        m = self.m
        i = i - (m - 1)
        early = lax.select(self.outer, 0, 1)
        late = i - early
        part = lax.div(lax.max(late, 0), m)
        near = jnp.logical_or(late < 0, part == 2)
        one = part == lax.select(self.outer, 1, 0)
        j = lax.select(near, lax.select(late < 0, i, i - 2 * m), late - part * m)
        one = jnp.logical_and(one, late >= 0)
        back = lax.select(near, lax.select(j == 0, m // 2 - 1, m - j - lax.div(m // 2 - 1 + j, m)), m - 1 - j)
        j = lax.select(jnp.logical_or(self.outer, one), j, back)
        base = lax.select(one, self.one, self.far)
        base = lax.select(near, self.near, base)
        inside = i < 0
        base = lax.select(inside, self.me, base)
        j = lax.select(inside, i + m, j)
        peer, bit = base, 1
        while bit < m:
            step = (1 - 2 * lax.rem(lax.div(self.me, bit), 2)) * bit
            peer = peer + step * lax.rem(lax.div(j, bit), 2)
            bit *= 2
        return peer


def ratio(scores, values, keys_left):
    keys = lax.broadcasted_iota(jnp.int32, scores.shape, 0)
    scores = jnp.where(keys < keys_left, scores, masked_score)
    highest = jnp.max(scores, axis=0, keepdims=True)
    factor = math.log2(math.e) / math.sqrt(HEAD_SIZE)
    weights = jnp.exp2((scores - highest) * factor)
    return jnp.sum(weights * values, axis=0, keepdims=True) / jnp.sum(
        weights, axis=0, keepdims=True
    )


def kernel(
    n, dims,
    stored_in, sources_in, lengths_in, direct_in, channel_in, cq, ts, tq, cs,
    out,
    stored, sources, lengths, table, direct_r, channel_r,
    cq_buf, ts_buf, tq_buf, v_buf, k_buf, u_out, u_buf, spread, owners, ud, rd, sel, score, owned, owned_count, dsum, owns, r_out, r_buf,
    in_sem, cq_sem, ks, kr, us, rs, rr, ready, both,
):
    T, S, I, J, H, G = dims
    C = T * S
    rpp = C // n
    hg = H // G
    D = HEAD_SIZE
    me = lax.axis_index(AXIS)

    loads = [
        pltpu.make_async_copy(cs.at[:, :, :, pl.ds(G * D, G * D)], v_buf, in_sem.at[0]),
        pltpu.make_async_copy(
            cs.at[me, :, :, pl.ds(0, G * D)], k_buf.at[me], in_sem.at[1]
        ),
        pltpu.make_async_copy(ts, ts_buf, in_sem.at[2]),
        pltpu.make_async_copy(tq, tq_buf, in_sem.at[3]),
        pltpu.make_async_copy(channel_in, channel_r, in_sem.at[4]),
        pltpu.make_async_copy(direct_in, direct_r, in_sem.at[5]),
        pltpu.make_async_copy(stored_in, stored, in_sem.at[6]),
        pltpu.make_async_copy(sources_in, sources, in_sem.at[7]),
        pltpu.make_async_copy(lengths_in, lengths, in_sem.at[8]),
        pltpu.make_async_copy(stored_in, owned, in_sem.at[9]),
        pltpu.make_async_copy(sources_in, owned_count, in_sem.at[10]),
    ]
    def cq_copy(t):
        return pltpu.make_async_copy(cq.at[t], cq_buf.at[t], cq_sem.at[t])

    barrier = pltpu.get_barrier_semaphore()
    peers = Peers(me, n)
    m = n // 4
    last = peers.quarter == 3

    def say(peer, semaphore):
        pl.semaphore_signal(
            semaphore, inc=1, device_id={AXIS: peer}, device_id_type=MESH
        )

    opens = peers.quarter == 0
    middle = jnp.logical_not(jnp.logical_or(opens, last))
    cross = peers.at(peers.two) + peers.at(peers.three)

    half = m // 2
    ahead = lax.rem(lax.div(me, half), 2) == 0
    first = jnp.logical_and(middle, ahead)
    second = jnp.logical_and(middle, jnp.logical_not(ahead))
    across = [base + step for base in (peers.three, me) for step in peers.steps[half:]]

    @pl.when(middle)
    def _():
        for peer in peers.at(peers.three)[:half] + peers.at(peers.one) + peers.at(peers.two):
            say(peer, barrier)
        for peer in peers.inside()[: half - 1]:
            say(peer, barrier)

    @pl.when(first)
    def _():
        for peer in across:
            say(peer, barrier)

    @pl.when(opens)
    def _():
        for peer in peers.at(peers.three):
            say(peer, barrier)

    @pl.when(jnp.logical_not(middle))
    def _():
        for peer in peers.inside():
            say(peer, barrier)

    for load in loads[4:]:
        load.start()
    loads[0].start()
    loads[2].start()
    cq_copy(0).start()

    def k_copy(p, slot):
        return pltpu.make_async_remote_copy(
            src_ref=cs.at[p, :, :, pl.ds(0, G * D)],
            dst_ref=k_buf.at[slot], send_sem=ks, recv_sem=kr.at[slot],
            device_id={AXIS: p}, device_id_type=MESH,
        )

    def u_copy(p, slot):
        return pltpu.make_async_remote_copy(
            src_ref=u_out.at[p], dst_ref=u_buf.at[slot], send_sem=us,
            recv_sem=kr.at[slot], device_id={AXIS: p}, device_id_type=MESH,
        )

    def r_copy(p, slot):
        return pltpu.make_async_remote_copy(
            src_ref=r_out.at[p], dst_ref=r_buf.at[slot], send_sem=rs,
            recv_sem=rr, device_id={AXIS: p}, device_id_type=MESH,
        )

    @pl.when(last)
    def _():
        pl.semaphore_wait(barrier, n - 1)
        for peer in cross + peers.at(peers.one):
            say(peer, ready)

    @pl.when(opens)
    def _():
        pl.semaphore_wait(barrier, n - 1 - m)
        for peer in peers.at(peers.one) + peers.at(peers.two):
            say(peer, ready)

    @pl.when(first)
    def _():
        pl.semaphore_wait(barrier, m - 1)

    @pl.when(second)
    def _():
        pl.semaphore_wait(barrier, 2 * m - 1)
        for peer in across:
            say(peer, ready)

    far = peers.at(peers.far)
    near = [
        peers.near + lax.select(peers.outer, peers.steps[m - 1 - k], peers.steps[peers.place(k)])
        for k in range(m)
    ]
    k_copy(near[0], me).start()

    @pl.when(peers.outer)
    def _():
        k_copy(near[1], me).start()

    loads[1].start()
    for t in range(1, T):
        cq_copy(t).start()
    loads[3].start()

    wide = u_out.shape[2]
    head_id = lax.broadcasted_iota(jnp.int32, (H, D), 0)
    rows_r = jnp.zeros((H, D), jnp.float32)
    loads[4].wait()
    for h in range(H):
        row = channel_r[h * D : (h + 1) * D].astype(jnp.float32).reshape(1, D)
        rows_r = jnp.where(head_id == h, row, rows_r)
    rows_r = jnp.concatenate([rows_r.astype(jnp.bfloat16)] * (wide // H), axis=0)
    row_id = lax.broadcasted_iota(jnp.int32, (wide, D), 0)
    loads[0].wait()
    u = None
    for r in range(rpp):
        for g in range(G):
            weights = jnp.where(
                row_id // hg == r * G + g, rows_r, jnp.zeros_like(rows_r)
            )
            values = v_buf[:, r, :, g * D : (g + 1) * D]
            values = values.reshape(n * I, D)
            part = dot_nt(values, weights)
            u = part if u is None else u + part
    turn = lax.rem(lax.broadcasted_iota(jnp.int32, u.shape, 1), hg)
    for q in range(1, hg):
        error = u - u.astype(jnp.bfloat16).astype(jnp.float32)
        u = jnp.where(turn == q, u + pltpu.roll(error, 1, 1), u)
    u_out[...] = u.astype(jnp.bfloat16).reshape(n, I, wide)

    lane = lax.broadcasted_iota(jnp.int32, (hg * J, wide), 1)
    head = lax.broadcasted_iota(jnp.int32, (hg * J, wide), 0) // J
    sel[...] = jnp.where(lax.rem(lane, hg) == head, 1.0, 0.0).astype(jnp.bfloat16)

    @pl.when(opens)
    def _():
        pl.semaphore_wait(ready, m)

    @pl.when(first)
    def _():
        pl.semaphore_wait(ready, 3 * m)

    @pl.when(second)
    def _():
        pl.semaphore_wait(ready, 2 * m)

    other = peers.inside() + peers.at(peers.one)
    for peer in near[:2] + far + near[2:] + other:
        u_copy(peer, me).start()
    for peer in far:
        k_copy(peer, me).start()

    @pl.when(jnp.logical_not(peers.outer))
    def _():
        k_copy(near[1], me).start()

    for peer in near[2:] + other:
        k_copy(peer, me).start()

    rows = S * I
    slot = lax.broadcasted_iota(jnp.int32, (1, rows), 1) // I
    for load in loads[5:]:
        load.wait()
    for t in range(T):
        held = jnp.zeros((1, rows), jnp.int32)
        count = jnp.zeros((1, rows), jnp.int32)
        for c in range(S):
            held = jnp.where(slot == c, stored[t, c], held)
            count = jnp.where(slot == c, sources[t, c], count)
        owners[t : t + 1, :] = held
        spread[t : t + 1, :] = count

    loads[2].wait()
    for g in range(G):
        states = ts_buf[:, :, (G + g) * D : (G + g + 1) * D].reshape(T * J, D)
        for q in range(hg):
            h = g * hg + q
            rd[q * rows : (q + 1) * rows, :] = jnp.broadcast_to(
                direct_r[h * D : (h + 1) * D].astype(jnp.float32).reshape(1, D), (rows, D)
            ).astype(jnp.bfloat16)
        ud[g] = dot_nt(states, rd[...])

    held = owned[...]
    target = lax.broadcasted_iota(jnp.int32, (T, S), 0)
    target_counts = jnp.zeros((T, S), jnp.int32)
    for t in range(T):
        target_counts = jnp.where(target == t, lengths[t], target_counts)
    base, step = 1 << J.bit_length(), 1 << (T - 1).bit_length()
    codes = (owned_count[...] * base + target_counts) * step + target
    for v in range(C):
        table[v] = jnp.max(jnp.where(held == v, codes, 0))

    token = lax.rem(lax.broadcasted_iota(jnp.int32, (1, rows), 1), I)

    def direct(t, carry):
        cq_copy(t).wait()
        total = jnp.zeros((1, hg * rows), jnp.float32)
        for g in range(G):
            queries = jnp.concatenate(
                [
                    cq_buf[t, :, (g * hg + q) * D : (g * hg + q + 1) * D]
                    for q in range(hg)
                ],
                axis=0,
            )
            scores = dot_nt(ts_buf[t, :, g * D : (g + 1) * D], queries)
            values = ud[g, pl.ds(pl.multiple_of(t * J, J), J), :]
            total = total + ratio(scores, values, lengths[t])
        tokens = total[:, 0:rows]
        for q in range(1, hg):
            tokens = tokens + total[:, q * rows : (q + 1) * rows]
        count = spread[pl.ds(t, 1), :]
        dsum[pl.ds(t, 1), :] = jnp.where(token < count, tokens, 0.0) / count.astype(jnp.float32)
        return carry

    lax.fori_loop(0, T, direct, 0)

    loads[3].wait()
    lanes = out.shape[0]
    direct_sums = dsum[...]
    owner = owners[...]
    rows_of = wide // rpp
    spot = lax.broadcasted_iota(jnp.int32, (T, wide), 1)
    for p in range(n):
        own = jnp.zeros((T, wide), jnp.float32)
        for r in range(rpp):
            part = jnp.where(owner == p * rpp + r, direct_sums, 0.0)
            part = jnp.sum(part, axis=1, keepdims=True)
            own = jnp.where(spot == r * rows_of, part, own)
        owns[p] = own
    RG = rpp * G
    key = lax.broadcasted_iota(jnp.int32, (I, hg * J), 0)
    row_of = lax.broadcasted_iota(jnp.int32, (RG, hg * J), 0) // G
    position = lax.rem(lax.broadcasted_iota(jnp.int32, (RG, hg * J), 1), J)
    row_of_sum = lax.broadcasted_iota(jnp.int32, (RG, wide), 0)
    own_lanes = lax.broadcasted_iota(jnp.int32, (RG, wide), 1) // hg == row_of_sum
    factor = math.log2(math.e) / math.sqrt(D)

    def lookup(p):
        targets, counts = [], []
        limits = jnp.zeros((RG, hg * J), jnp.int32)
        for r in range(rpp):
            code = table[p * rpp + r]
            targets.append(lax.rem(code, step))
            counts.append(lax.div(code, base * step))
            limits = jnp.where(row_of == r, lax.rem(lax.div(code, step), base), limits)
        kept = position < limits
        shares = jnp.where(own_lanes, 1.0 / limits[:, :wide].astype(jnp.float32), 0.0)
        own = jnp.sum(owns[p], axis=0, keepdims=True)
        return targets, counts, kept, shares, own

    def block(p, found):
        targets, counts, kept, shares, own = found
        for r in range(rpp):
            t = targets[r]
            source_count = counts[r]
            usable = key < source_count
            for g in range(G):
                queries = jnp.concatenate(
                    [
                        tq_buf[t, :, (g * hg + q) * D : (g * hg + q + 1) * D]
                        for q in range(hg)
                    ],
                    axis=0,
                )
                scores = dot_nt(k_buf[p, r, :, g * D : (g + 1) * D], queries)
                scores = jnp.where(usable, scores, masked_score)
                for c in range(0, hg * J, 128):
                    score[c // 128, pl.ds(r * G + g, I, stride=RG), :] = scores[:, c : c + 128]
        def at(k):
            return jnp.concatenate(
                [score[c, k * RG : (k + 1) * RG, :] for c in range(hg * J // 128)], axis=1
            )
        highest = at(0)
        for k in range(1, I):
            highest = jnp.maximum(highest, at(k))
        weights = [jnp.exp2((at(k) - highest) * factor) for k in range(I)]
        total = weights[0]
        for k in range(1, I):
            total = total + weights[k]
        scale = jnp.where(kept, 1.0 / total, 0.0)
        probs = jnp.concatenate(
            [(w * scale).astype(jnp.bfloat16) for w in weights], axis=0
        )
        sums = jnp.dot(probs, sel[...], preferred_element_type=jnp.float32)
        u = u_buf[p].astype(jnp.float32)
        mixed = sums[0:RG] * u[0:1]
        for k in range(1, I):
            mixed = mixed + sums[k * RG : (k + 1) * RG] * u[k : k + 1]
        return jnp.sum(mixed * shares, axis=0, keepdims=True) + own

    u_buf[me] = u_out[me]
    loads[1].wait()
    r_buf[me] = block(me, lookup(me))

    def channel_step(i, carry):
        p = peers.arrival(i)
        found = lookup(p)
        pltpu.make_async_copy(both, both, kr.at[p]).wait()
        r_out[p] = block(p, found)
        r_copy(p, me).start()

        return carry

    lax.fori_loop(0, n - 1, channel_step, 0)

    def settle(buffer, semaphore):
        rest = buffer.at[pl.ds(0, n - 1)]
        pltpu.make_async_copy(rest, rest, semaphore).wait()

    settle(r_buf, rr)
    settle(k_buf, ks)
    settle(u_buf, us)
    settle(r_buf, rs)
    sums = r_buf[...].reshape(n, wide)
    part = lax.broadcasted_iota(jnp.int32, (n, wide), 1) // rows_of
    place = lax.broadcasted_iota(jnp.int32, (n, lanes), 1)
    source = lax.broadcasted_iota(jnp.int32, (n, lanes), 0)
    result = jnp.zeros((n, lanes), jnp.float32)
    for r in range(rpp):
        value = jnp.sum(jnp.where(part == r, sums, 0.0), axis=1, keepdims=True)
        result = jnp.where(place == source * rpp + r, value, result)
    out[...] = jnp.sum(result, axis=0)


def on_device(
    n,
    candidate_queries,
    target_states,
    target_queries,
    candidate_states,
    target_length,
    candidate_length,
    candidate_row,
    direct_readout,
    channel_readout,
):
    T, S, I, QW = candidate_queries.shape
    J = target_states.shape[1]
    H = QW // HEAD_SIZE
    G = target_states.shape[2] // (2 * HEAD_SIZE)
    C = T * S
    rpp = C // n
    hg = H // G
    wide = max(128, rpp * H)
    lanes = -(-C // 128) * 128
    bf, f32 = jnp.bfloat16, jnp.float32
    vmem, smem = pltpu.VMEM, pltpu.SMEM
    anywhere = pl.BlockSpec(memory_space=pl.ANY)
    dma = pltpu.SemaphoreType.DMA
    found = pl.pallas_call(
        functools.partial(kernel, n, (T, S, I, J, H, G)),
        out_shape=jax.ShapeDtypeStruct((C,), f32),
        in_specs=[
            anywhere, anywhere, anywhere, anywhere, anywhere,
            anywhere, anywhere, anywhere, anywhere,
        ],
        out_specs=pl.BlockSpec(memory_space=vmem),
        scratch_shapes=[
            smem((T, S), jnp.int32),
            smem((T, S), jnp.int32),
            smem((T,), jnp.int32),
            smem((C,), jnp.int32),
            vmem((QW,), bf),
            vmem((QW,), bf),
            vmem((T, S * I, QW), bf),
            vmem(target_states.shape, bf),
            vmem(target_queries.shape, bf),
            vmem((n, rpp, I, G * HEAD_SIZE), bf),
            vmem((n, rpp, I, G * HEAD_SIZE), bf),
            vmem((n, I, wide), bf),
            vmem((n, I, wide), bf),
            vmem((T, S * I), jnp.int32),
            vmem((T, S * I), jnp.int32),
            vmem((G, T * J, hg * S * I), f32),
            vmem((hg * S * I, HEAD_SIZE), bf),
            vmem((hg * J, wide), bf),
            vmem((hg * J // 128, I * rpp * G, 128), f32),
            vmem((T, S), jnp.int32),
            vmem((T, S), jnp.int32),
            vmem((T, S * I), f32),
            vmem((n, T, wide), f32),
            vmem((n, 1, wide), f32),
            vmem((n, 1, wide), f32),
            dma((11,)), dma((T,)),
            dma, dma((n,)), dma, dma, dma,
            pltpu.SemaphoreType.REGULAR,
            vmem((rpp * I * G + I * wide // HEAD_SIZE, HEAD_SIZE), bf),
        ],
        compiler_params=pltpu.CompilerParams(
            collective_id=0, has_side_effects=True, vmem_limit_bytes=56553472
        ),
    )(
        candidate_row, candidate_length, target_length,
        direct_readout, channel_readout,
        candidate_queries.reshape(T, S * I, QW),
        target_states, target_queries,
        candidate_states.reshape(n, rpp, I, 2 * G * HEAD_SIZE),
    )
    return found


def solution(mesh):
    in_specs = (
        P(("group", "dp"), None, None, None),
        P(("group", "dp"), None, None),
        P(("group", "dp"), None, None),
        P(("group", "dp"), None, None),
        P(("group", "dp")),
        P(("group", "dp"), None),
        P(("group", "dp"), None),
        P(),
        P(),
    )
    return jax.shard_map(
        functools.partial(on_device, mesh.shape[AXIS]),
        mesh=mesh, in_specs=in_specs, out_specs=P(("group", "dp")), check_vma=False,
    )
```
